256 devices in a mesh: band: 8 (over z), ord: 32 (over x, y, core).
Axes of the slice: x: 4, y: 4, z: 8, core: 2. Of those that a mesh axis runs over, the one named last changes fastest.
Arguments:
- density: bfloat16 [8, 128, 256, 512], P('band', None, 'ord'), may hold values from -6 to 6
- degree_weights: float32 [8, 256], P('band'), may hold values from 0.25 to 1
- row_orders: int32 [256], replicated, may hold values from 0 to 255, each once
- target_cycles: int32 [128], replicated, may hold values from 0 to 255, as said below
Outputs:
- coeffs: bfloat16 [8, 256, 128, 2, 256], P('band', 'ord')
- potential: float32 [128, 128, 512], P('band', 'ord')
The draws below stay inside these ranges and needn't reach their ends.
Inputs may be any that keep to these rules, and one draw needn't show every extreme that they name: `row_orders`: each order appears once. `target_cycles`: 128 distinct cycle indices.
All inputs are finite; a program needn't handle non-finite values.
Results may differ from the reference program's by a relative error of at most 0.0095.
Values may be sent and summed in bfloat16 or wider, within the bound.
No kernel may reach another device: no remote copies, remote signals or barrier semaphores. Data moves between devices by JAX's collectives and lax.ppermute only.
A program may use at most 64 MiB of HBM per device.

```python
import math
import jax
import jax.numpy as jnp
from jax import lax

ORDERS = 256
LATITUDES = 256
LONGITUDES = 512
TARGETS = 128
DENSITIES = 128
GROUPS = 8


def draw_target_cycles(key, part):
    inner = jax.random.permutation(key, LATITUDES - 2)[:TARGETS - 2] + 1
    chosen = jnp.concatenate([jnp.array([0, LATITUDES - 1], jnp.int32), inner.astype(jnp.int32)])
    return jax.random.permutation(jax.random.fold_in(key, 7), chosen).astype(jnp.int32)


def block_scale(own_key, extent, pieces, smallest, high):
    gain = 1.0
    for position, blocks in pieces:
        heights = jax.random.uniform(jax.random.fold_in(jax.random.fold_in(own_key, 6), position), (blocks,), jnp.float32, smallest / len(pieces), high / len(pieces))
        gain = gain * jnp.repeat(jnp.exp(heights), extent[position] // blocks).reshape((-1,) + (1,) * (len(extent) - 1 - position))
    return gain


def normal_values(own_key, extent, spread, reach, shards=(), kind=jnp.bfloat16):
    level = block_scale(own_key, extent, shards, -0.22, 0.18) if shards else 1.0
    values = jax.random.normal(own_key, extent, jnp.float32) * spread * level
    return jnp.minimum(jnp.maximum(values, -reach), reach).astype(kind)


def setup_inputs(seed: int = 0) -> dict:
    key_of = jax.random.split(jax.random.key(seed), 5)
    density = normal_values(key_of[0], (GROUPS, DENSITIES, LATITUDES, LONGITUDES), 1.0, 6.0, ((0, 8), (2, 32)))
    degree_weights = jnp.clip(jnp.exp(math.log(1.0) - 1.3862944 * jax.random.uniform(key_of[1], (GROUPS, ORDERS), jnp.float32) ** block_scale(key_of[1], (GROUPS, ORDERS), ((0, 8),), -0.2, 0.2)), 0.25, 1.0)
    row_orders = jax.random.permutation(key_of[2], ORDERS).astype(jnp.int32)
    target_cycles = draw_target_cycles(jax.random.fold_in(key_of[4], 71), 0)
    return {"density": density, "degree_weights": degree_weights, "row_orders": row_orders, "target_cycles": target_cycles}


def rounded_values(values):
    return lax.optimization_barrier(values.astype(jnp.bfloat16)).astype(jnp.float32)

def cycle_grid(cycle_count):
    centers = (jnp.arange(cycle_count, dtype=jnp.float32) + 0.5) * (math.pi / cycle_count)
    return (jnp.cos(centers), jnp.sin(centers))

def legendre_rows(order_vals, cycle_count, degree_count):
    cosines, sine_vals = cycle_grid(cycle_count)
    steps_f = jnp.arange(1, degree_count, dtype=jnp.float32)
    log_terms = jnp.log((2.0 * steps_f + 1.0) / (2.0 * steps_f))
    gamma_terms = lax.optimization_barrier(jnp.sum(jnp.where(steps_f[None, :] <= order_vals[:, None], log_terms[None, :], 0.0), axis=1))
    log_start = 0.5 * (math.log(1.0 / (4.0 * math.pi)) + gamma_terms)[:, None] + order_vals[:, None] * jnp.log(sine_vals)[None, :]
    shift_vals = jnp.clip(-log_start - 40.0, 0.0, 80.0)
    sectoral_terms = jnp.exp(log_start + shift_vals)
    orders_col = order_vals[:, None]

    def advance(carry, degree_f):
        previous, earlier = carry
        denom = jnp.maximum(degree_f * degree_f - orders_col * orders_col, 1.0)
        growth = jnp.sqrt(jnp.maximum(4.0 * degree_f * degree_f - 1.0, 0.0) / denom)
        lower = degree_f - 1.0
        damping = jnp.sqrt(jnp.maximum(lower * lower - orders_col * orders_col, 0.0) / jnp.maximum(4.0 * lower * lower - 1.0, 1.0))
        grown = growth * (cosines[None, :] * previous - damping * earlier)
        current = jnp.where(degree_f < orders_col, 0.0, jnp.where(degree_f == orders_col, sectoral_terms, grown))
        return ((current, previous), current)
    empty = jnp.zeros(sectoral_terms.shape, jnp.float32)
    _, table = lax.scan(advance, (empty, empty), jnp.arange(degree_count, dtype=jnp.float32))
    return table * jnp.exp(-shift_vals)[None, :, :]

def forward_table(orders, lon_count, lat_count):
    lon_index = jnp.arange(lon_count, dtype=jnp.int32)
    turns = lon_index[:, None] * orders[None, :] % lon_count
    phases = turns.astype(jnp.float32) * (2.0 * math.pi / lon_count)
    factor = 2.0 * math.pi / lon_count * math.sqrt(lat_count * lon_count / (4.0 * math.pi))
    return jnp.stack([factor * jnp.cos(phases), -factor * jnp.sin(phases)], axis=1).astype(jnp.bfloat16)

def inverse_table(orders, lon_count, lat_count):
    lon_index = jnp.arange(lon_count, dtype=jnp.int32)
    turns = orders[:, None] * lon_index[None, :] % lon_count
    phases = turns.astype(jnp.float32) * (2.0 * math.pi / lon_count)
    factor = jnp.where(orders == 0, 1.0, 2.0).astype(jnp.float32)[:, None] / math.sqrt(lat_count * lon_count / (4.0 * math.pi))
    return jnp.stack([factor * jnp.cos(phases), -factor * jnp.sin(phases)], axis=1).astype(jnp.bfloat16)

def reference(density, degree_weights, row_orders, target_cycles):
    cosines, sine_vals = cycle_grid(LATITUDES)
    cycle_weights = math.pi / LATITUDES * sine_vals
    all_orders = jnp.arange(ORDERS, dtype=jnp.int32)
    legendre = legendre_rows(all_orders.astype(jnp.float32), LATITUDES, ORDERS)
    analysis = (legendre * cycle_weights[None, None, :]).astype(jnp.bfloat16).astype(jnp.float32)
    synthesis_result = jnp.take(legendre, target_cycles.astype(jnp.int32), axis=2).astype(jnp.bfloat16).astype(jnp.float32)
    forward = forward_table(all_orders, LONGITUDES, LATITUDES).astype(jnp.float32)
    inverse = inverse_table(all_orders, LONGITUDES, LATITUDES).astype(jnp.float32)
    potential = jnp.zeros((TARGETS, DENSITIES, LONGITUDES), jnp.float32)
    coefficient_entries = []
    for group in range(GROUPS):
        spectra = rounded_values(jnp.einsum('qjk,kcm->mqcj', density[group].astype(jnp.float32), forward))
        harmonic = jnp.einsum('mqcj,lmj->mqcl', spectra, analysis).astype(jnp.bfloat16)
        coefficient_entries.append(jnp.take(harmonic, row_orders.astype(jnp.int32), axis=0))
        scaled_values = rounded_values(harmonic.astype(jnp.float32) * degree_weights[group][None, None, None, :])
        harmonic_modes = rounded_values(jnp.einsum('zihp,pzx->zihx', scaled_values, synthesis_result))
        potential = potential + jnp.einsum('mqcr,mck->rqk', harmonic_modes, inverse)
    return (jnp.stack(coefficient_entries), potential)
```

```python
import math

import numpy as np
import jax
import jax.numpy as jnp
from jax import lax
from jax.experimental import pallas as pl
from jax.experimental.pallas import tpu as pltpu
from jax.sharding import PartitionSpec as P

F32 = jnp.float32
BF16 = jnp.bfloat16
NN = (((1,), (0,)), ((), ()))
NT = (((1,), (1,)), ((), ()))
TN = (((0,), (0,)), ((), ()))


def dot(a, b, dims=NN):
    return lax.dot_general(a, b, dims, preferred_element_type=F32)


def trig_tables(order_count, lon_count, lat_count):
    turns = np.arange(order_count)[:, None] * np.arange(lon_count)[None, :] % lon_count
    phases = turns * (2.0 * math.pi / lon_count)
    gain = math.sqrt(lat_count * lon_count / (4.0 * math.pi))
    waves = np.concatenate([np.cos(phases), -np.sin(phases)], axis=1)
    forward = waves * (2.0 * math.pi / lon_count * gain)
    twice = np.where(np.arange(order_count) == 0, 1.0, 2.0)[:, None]
    inverse = waves * twice / gain
    kind = jnp.dtype(BF16)
    return forward.astype(np.float32).astype(kind), inverse.astype(np.float32).astype(kind)


def iota(shape, axis):
    return lax.broadcasted_iota(jnp.int32, shape, axis)


def one_hot(hit):
    return jnp.where(hit, 1.0, 0.0).astype(BF16)


def swap_matrix(outer, inner):
    n = outer * inner
    row, col = iota((n, n), 0), iota((n, n), 1)
    return one_hot(col == (row % inner) * outer + row // inner)


def forward_kernel(orders_ref, density_ref, table_ref, out_ref, turned_ref):
    picks = one_hot(iota((256, 256), 0) == orders_ref[...])
    rows = dot(picks, table_ref[...], TN)
    cos_rows = rows[:, :512].reshape(32, 8, 512)
    sin_rows = rows[:, 512:].reshape(32, 8, 512)
    forward = jnp.stack([cos_rows, sin_rows], axis=1).reshape(512, 512).astype(BF16)
    swap = swap_matrix(8, 32)
    for b in range(4):
        part = dot(swap, density_ref[b * 256 : (b + 1) * 256, :]).astype(BF16)
        turned_ref[:, b * 32 : (b + 1) * 32, :] = part.reshape(8, 32, 512)
    for j in range(0, 8, 2):
        lanes = turned_ref[j : j + 2].reshape(256, 512)
        part = dot(forward, lanes, NT).astype(BF16)
        for h in range(2):
            block = part[:, h * 128 : (h + 1) * 128].reshape(32, 16, 128)
            out_ref[:, (j + h) * 16 : (j + h + 1) * 16, :] = block


def table_kernel(own_ref, orders_ref, target_ref, grid_ref, inverse_ref,
                 analysis_ref, synthesis_ref, inv_ref, legendre_ref, rows_ref):
    sub = iota((8, 256), 0)
    order = jnp.zeros((8, 256), F32)
    for i in range(8):
        order = jnp.where(sub == i, own_ref[i].astype(F32), order)
    cosines = jnp.broadcast_to(grid_ref[0:1, :], (8, 256))
    log_sines = jnp.log(grid_ref[1:2, :])
    weights = grid_ref[2:3, :]
    steps = iota((8, 256), 1).astype(F32)
    safe = jnp.maximum(steps, 1.0)
    log_terms = jnp.log((2.0 * safe + 1.0) / (2.0 * safe))
    counted = (steps >= 1.0) & (steps <= order)
    gamma = jnp.sum(jnp.where(counted, log_terms, 0.0), axis=1, keepdims=True)
    log_start = 0.5 * (math.log(1.0 / (4.0 * math.pi)) + gamma) + order * log_sines
    shift = jnp.clip(-log_start - 40.0, 0.0, 80.0)
    sectoral = jnp.exp(log_start + shift)
    unshift = jnp.exp(-shift)
    half = order[:, :128]
    half_sq = half * half

    def wide(a):
        return jnp.concatenate([a, a], axis=1)

    def advance(step, carry):
        previous, earlier = carry
        degree = jnp.full((8, 128), step, jnp.int32).astype(F32)
        square = degree * degree
        growth = jnp.sqrt(
            jnp.maximum(4.0 * square - 1.0, 0.0) / jnp.maximum(square - half_sq, 1.0)
        )
        lower = degree - 1.0
        low_sq = lower * lower
        damping = jnp.sqrt(
            jnp.maximum(low_sq - half_sq, 0.0) / jnp.maximum(4.0 * low_sq - 1.0, 1.0)
        )
        grown = wide(growth) * (cosines * previous - wide(damping) * earlier)
        wide_degree = wide(degree)
        current = jnp.where(
            wide_degree < order, 0.0, jnp.where(wide_degree == order, sectoral, grown)
        )
        final = current * unshift
        rows = pl.ds(pl.multiple_of(step * 8, 8), 8)
        legendre_ref[0, rows, :] = final[:, :128]
        legendre_ref[1, rows, :] = final[:, 128:]
        return current, previous

    empty = sectoral * 0.0
    lax.fori_loop(0, 256, advance, (empty, empty), unroll=8)

    hits = jnp.where(iota((256, 128), 0) == target_ref[...], 1.0, 0.0)
    picks = hits.T.astype(BF16)
    for i in range(8):
        halves = [legendre_ref[h, pl.ds(i, 256, stride=8), :] for h in range(2)]
        own = jnp.concatenate(halves, axis=1)
        analysis_ref[i] = (own * weights).astype(BF16)
        synthesis_ref[i] = dot(picks, own.astype(BF16), NT).astype(BF16)

    places = one_hot(iota((256, 256), 0) == orders_ref[...])
    rows = dot(places, inverse_ref[...], TN)
    for c in range(8):
        rows_ref[c] = rows[:, c * 128 : (c + 1) * 128]
    for i in range(8):
        for c in range(8):
            own = rows_ref[c, pl.ds(i, 32, stride=8), :].astype(BF16)
            top = i * 64 + c // 4 * 32
            inv_ref[top : top + 32, c % 4 * 128 : (c % 4 + 1) * 128] = own


def order_kernel(spectra_ref, analysis_ref, synthesis_ref, weights_ref,
                 coeffs_ref, out_ref, cycles_ref, modes_ref):
    swap = swap_matrix(16, 16)
    for b in range(0, 16, 2):
        first = spectra_ref[b * 256 : (b + 1) * 256, :]
        second = spectra_ref[(b + 1) * 256 : (b + 2) * 256, :]
        both = dot(swap, jnp.concatenate([first, second], axis=1)).astype(BF16)
        cycles_ref[:, b * 16 : (b + 1) * 16, :] = both[:, :128].reshape(16, 16, 128)
        cycles_ref[:, (b + 1) * 16 : (b + 2) * 16, :] = both[:, 128:].reshape(16, 16, 128)
    scale = jnp.broadcast_to(weights_ref[...], (128, 256)).T
    scale = jnp.concatenate([scale, scale], axis=1)
    row, col = iota((256, 256), 0), iota((256, 256), 1)
    interleave = one_hot(col == (row % 2) * 128 + row // 2)
    deal = one_hot(col == (row // 4 % 2) * 128 + row // 8 * 4 + row % 4)
    for i in range(8):
        lanes = jnp.concatenate([cycles_ref[i], cycles_ref[8 + i]], axis=1)
        harmonic = dot(analysis_ref[i], lanes).astype(BF16)
        coeffs_ref[i] = dot(interleave, harmonic, NT).astype(BF16)
        scaled = (harmonic.astype(F32) * scale).astype(BF16)
        modes = dot(synthesis_ref[i], scaled).astype(BF16)
        modes_ref[:, i * 16 : (i + 1) * 16, :] = modes.reshape(8, 16, 256)
    for b in range(8):
        block = dot(deal, modes_ref[b], NT)
        out_ref[b * 256 : (b + 1) * 256, :] = block.astype(BF16)


def inverse_kernel(modes_ref, inv_ref, out_ref, sum_ref):
    total = modes_ref[0:256, :].astype(F32)
    for g in range(1, 8):
        total = total + modes_ref[g * 256 : (g + 1) * 256, :].astype(F32)
    sum_ref[...] = total
    blocks = []
    for q in range(4):
        parts = [sum_ref[pl.ds(c * 4 + q, 32, stride=8), :] for c in range(2)]
        turned = jnp.concatenate(parts, axis=0).T
        own = [turned[i * 16 : (i + 1) * 16, :] for i in range(8)]
        blocks.append(jnp.concatenate(own, axis=1))
    left = jnp.concatenate(blocks, axis=0).astype(BF16)
    result = dot(left, inv_ref[...])
    for q in range(4):
        out_ref[:, q, :] = result[q * 16 : (q + 1) * 16, :]


def struct(shape, kind):
    return jax.ShapeDtypeStruct(shape, kind)


VMEM_SPEC = pl.BlockSpec(memory_space=pltpu.VMEM)
SMEM_SPEC = pl.BlockSpec(memory_space=pltpu.SMEM)


def local(density, degree_weights, row_orders, target_cycles):
    forward_trig, inverse_trig = trig_tables(256, 512, 256)
    orders_row = row_orders.reshape(1, 256)
    own_orders = lax.dynamic_slice_in_dim(row_orders, lax.axis_index("ord") * 8, 8)
    centers = (jnp.arange(256, dtype=F32) + 0.5) * (math.pi / 256)
    grid = jnp.stack([jnp.cos(centers), jnp.sin(centers), math.pi / 256 * jnp.sin(centers)])

    spectra = pl.pallas_call(
        forward_kernel,
        out_shape=struct((32, 128, 128), BF16),
        in_specs=[VMEM_SPEC] * 3,
        out_specs=VMEM_SPEC,
        scratch_shapes=[pltpu.VMEM((8, 128, 512), BF16)],
        name="forward",
    )(orders_row, density.reshape(1024, 512), jnp.asarray(forward_trig))
    by_order = lax.all_to_all(spectra, "ord", split_axis=0, concat_axis=0, tiled=True)

    analysis, synthesis, inverse_rows = pl.pallas_call(
        table_kernel,
        out_shape=(
            struct((8, 256, 256), BF16),
            struct((8, 128, 256), BF16),
            struct((512, 512), BF16),
        ),
        in_specs=[SMEM_SPEC] + [VMEM_SPEC] * 4,
        out_specs=(VMEM_SPEC,) * 3,
        scratch_shapes=[pltpu.VMEM((2, 2048, 128), F32), pltpu.VMEM((8, 256, 128), F32)],
        name="tables",
    )(own_orders, orders_row, target_cycles.reshape(1, 128), grid, jnp.asarray(inverse_trig))

    coeffs, modes = pl.pallas_call(
        order_kernel,
        out_shape=(struct((8, 256, 256), BF16), struct((2048, 128), BF16)),
        in_specs=[VMEM_SPEC] * 4,
        out_specs=(VMEM_SPEC,) * 2,
        scratch_shapes=[pltpu.VMEM((16, 256, 128), BF16), pltpu.VMEM((8, 128, 256), BF16)],
        name="orders",
    )(by_order.reshape(4096, 128), analysis, synthesis, degree_weights)

    arrived = lax.all_to_all(
        modes.reshape(256, 8, 128), ("band", "ord"), split_axis=0, concat_axis=0, tiled=True
    )
    potential = pl.pallas_call(
        inverse_kernel,
        out_shape=struct((16, 4, 512), F32),
        in_specs=[VMEM_SPEC] * 2,
        out_specs=VMEM_SPEC,
        scratch_shapes=[pltpu.VMEM((256, 128), F32)],
        name="inverse",
    )(arrived.reshape(2048, 128), inverse_rows)
    return coeffs.reshape(1, 8, 128, 2, 256), potential


def solution(mesh):
    in_specs = (P("band", None, "ord", None), P("band", None), P(), P())
    out_specs = (P("band", "ord", None, None, None), P("band", "ord", None))
    return jax.shard_map(local, mesh=mesh, in_specs=in_specs, out_specs=out_specs, check_vma=False)
```

```python
import math

import numpy as np
import jax
import jax.numpy as jnp
from jax import lax
from jax.experimental import pallas as pl
from jax.experimental.pallas import tpu as pltpu
from jax.sharding import PartitionSpec as P

F32 = jnp.float32
BF16 = jnp.bfloat16
NN = (((1,), (0,)), ((), ()))
NT = (((1,), (1,)), ((), ()))
TN = (((0,), (0,)), ((), ()))


def dot(a, b, dims=NN):
    return lax.dot_general(a, b, dims, preferred_element_type=F32)


def trig_tables(order_count, lon_count, lat_count):
    turns = np.arange(order_count)[:, None] * np.arange(lon_count)[None, :] % lon_count
    phases = turns * (2.0 * math.pi / lon_count)
    gain = math.sqrt(lat_count * lon_count / (4.0 * math.pi))
    waves = np.concatenate([np.cos(phases), -np.sin(phases)], axis=1)
    forward = waves * (2.0 * math.pi / lon_count * gain)
    twice = np.where(np.arange(order_count) == 0, 1.0, 2.0)[:, None]
    inverse = waves * twice / gain
    kind = jnp.dtype(BF16)
    return forward.astype(np.float32).astype(kind), inverse.astype(np.float32).astype(kind)


def iota(shape, axis):
    return lax.broadcasted_iota(jnp.int32, shape, axis)


def one_hot(hit):
    return jnp.where(hit, 1.0, 0.0).astype(BF16)


def swap_matrix(outer, inner):
    n = outer * inner
    row, col = iota((n, n), 0), iota((n, n), 1)
    return one_hot(col == (row % inner) * outer + row // inner)


def forward_kernel(orders_hbm, density_hbm, table_hbm, out_hbm,
                   orders_ref, density_ref, table_ref, turned_ref, out_ref,
                   orders_sem, table_sem, density_sem, out_sem):
    orders_copy = pltpu.make_async_copy(orders_hbm, orders_ref, orders_sem)
    orders_copy.start()
    table_copy = pltpu.make_async_copy(table_hbm, table_ref, table_sem)
    table_copy.start()
    copies = []
    for b in range(4):
        rows = pl.ds(b * 256, 256)
        copy = pltpu.make_async_copy(density_hbm.at[rows], density_ref.at[rows], density_sem.at[b])
        copy.start()
        copies.append(copy)
    orders_copy.wait()
    picks = one_hot(iota((256, 256), 0) == orders_ref[...])
    swap = swap_matrix(8, 32)
    table_copy.wait()
    rows = dot(picks, table_ref[...], TN)
    cos_rows = rows[:, :512].reshape(32, 8, 512)
    sin_rows = rows[:, 512:].reshape(32, 8, 512)
    forward = jnp.stack([cos_rows, sin_rows], axis=1).reshape(512, 512).astype(BF16)
    for b in range(4):
        copies[b].wait()
        part = dot(swap, density_ref[b * 256 : (b + 1) * 256, :]).astype(BF16)
        turned_ref[:, b * 32 : (b + 1) * 32, :] = part.reshape(8, 32, 512)
    sends = []
    for j in range(0, 8, 2):
        lanes = turned_ref[j : j + 2].reshape(256, 512)
        part = dot(forward, lanes, NT).astype(BF16)
        for h in range(2):
            block = part[:, h * 128 : (h + 1) * 128].reshape(32, 16, 128)
            out_ref[:, (j + h) * 16 : (j + h + 1) * 16, :] = block
        rows = pl.ds(j * 16, 32)
        send = pltpu.make_async_copy(out_ref.at[:, rows], out_hbm.at[:, rows], out_sem.at[j // 2])
        send.start()
        sends.append(send)
    for send in sends:
        send.wait()


def table_kernel(own_ref, orders_ref, target_ref, grid_ref, inverse_ref,
                 legendre_out_ref, inv_ref, legendre_ref, rows_ref):
    sub = iota((8, 256), 0)
    order = jnp.zeros((8, 256), F32)
    for i in range(8):
        order = jnp.where(sub == i, own_ref[i].astype(F32), order)
    cosines = jnp.broadcast_to(grid_ref[0:1, :], (8, 256))
    log_sines = jnp.log(grid_ref[1:2, :])
    weights = grid_ref[2:3, :]
    steps = iota((8, 256), 1).astype(F32)
    safe = jnp.maximum(steps, 1.0)
    log_terms = jnp.log((2.0 * safe + 1.0) / (2.0 * safe))
    counted = (steps >= 1.0) & (steps <= order)
    gamma = jnp.sum(jnp.where(counted, log_terms, 0.0), axis=1, keepdims=True)
    log_start = 0.5 * (math.log(1.0 / (4.0 * math.pi)) + gamma) + order * log_sines
    shift = jnp.clip(-log_start - 40.0, 0.0, 80.0)
    sectoral = jnp.exp(log_start + shift)
    unshift = jnp.exp(-shift)
    half = order[:, :128]
    half_sq = half * half

    def wide(a):
        return jnp.concatenate([a, a], axis=1)

    def advance(step, carry):
        previous, earlier = carry
        degree = jnp.full((8, 128), step, jnp.int32).astype(F32)
        square = degree * degree
        growth = jnp.sqrt(
            jnp.maximum(4.0 * square - 1.0, 0.0) / jnp.maximum(square - half_sq, 1.0)
        )
        lower = degree - 1.0
        low_sq = lower * lower
        damping = jnp.sqrt(
            jnp.maximum(low_sq - half_sq, 0.0) / jnp.maximum(4.0 * low_sq - 1.0, 1.0)
        )
        grown = wide(growth) * (cosines * previous - wide(damping) * earlier)
        wide_degree = wide(degree)
        current = jnp.where(
            wide_degree < order, 0.0, jnp.where(wide_degree == order, sectoral, grown)
        )
        final = current * unshift
        rows = pl.ds(pl.multiple_of(step * 8, 8), 8)
        legendre_ref[0, rows, :] = final[:, :128]
        legendre_ref[1, rows, :] = final[:, 128:]
        return current, previous

    empty = sectoral * 0.0
    lax.fori_loop(0, 256, advance, (empty, empty), unroll=8)

    hits = jnp.where(iota((256, 128), 0) == target_ref[...], 1.0, 0.0)
    picks = hits.T.astype(BF16)
    for i in range(8):
        halves = [legendre_ref[h, pl.ds(i, 256, stride=8), :] for h in range(2)]
        own = jnp.concatenate(halves, axis=1)
        legendre_out_ref[i, :256, :] = (own * weights).astype(BF16)
        legendre_out_ref[i, 256:, :] = dot(picks, own.astype(BF16), NT).astype(BF16)

    places = one_hot(iota((256, 256), 0) == orders_ref[...])
    rows = dot(places, inverse_ref[...], TN)
    for c in range(8):
        rows_ref[c] = rows[:, c * 128 : (c + 1) * 128]
    for i in range(8):
        for c in range(8):
            own = rows_ref[c, pl.ds(i, 32, stride=8), :].astype(BF16)
            top = i * 64 + c // 4 * 32
            inv_ref[top : top + 32, c % 4 * 128 : (c % 4 + 1) * 128] = own


def order_kernel(spectra_ref, legendre_ref, weights_ref,
                 harmonic_hbm, out_hbm, cycles_ref, modes_ref, harmonic_ref, out_ref,
                 harmonic_sem, out_sem):
    swap = swap_matrix(16, 16)
    for b in range(0, 16, 2):
        first = spectra_ref[b * 256 : (b + 1) * 256, :]
        second = spectra_ref[(b + 1) * 256 : (b + 2) * 256, :]
        both = dot(swap, jnp.concatenate([first, second], axis=1)).astype(BF16)
        cycles_ref[:, b * 16 : (b + 1) * 16, :] = both[:, :128].reshape(16, 16, 128)
        cycles_ref[:, (b + 1) * 16 : (b + 2) * 16, :] = both[:, 128:].reshape(16, 16, 128)
    scale = jnp.broadcast_to(weights_ref[...], (128, 256)).T
    scale = jnp.concatenate([scale, scale], axis=1)
    row, col = iota((256, 256), 0), iota((256, 256), 1)
    deal = one_hot(col == (row // 4 % 2) * 128 + row // 8 * 4 + row % 4)
    sends = []
    for i in range(8):
        lanes = jnp.concatenate([cycles_ref[i], cycles_ref[8 + i]], axis=1)
        harmonic = dot(legendre_ref[i, :256, :], lanes).astype(BF16)
        harmonic_ref[i] = harmonic
        send = pltpu.make_async_copy(harmonic_ref.at[i], harmonic_hbm.at[i], harmonic_sem.at[i])
        send.start()
        sends.append(send)
        scaled = (harmonic.astype(F32) * scale).astype(BF16)
        modes = dot(legendre_ref[i, 256:, :], scaled).astype(BF16)
        modes_ref[:, i * 16 : (i + 1) * 16, :] = modes.reshape(8, 16, 256)
    for b in range(8):
        block = dot(deal, modes_ref[b], NT)
        rows = pl.ds(b * 256, 256)
        out_ref[rows, :] = block.astype(BF16)
        send = pltpu.make_async_copy(out_ref.at[rows], out_hbm.at[rows], out_sem.at[b])
        send.start()
        sends.append(send)
    for send in sends:
        send.wait()


def coeffs_kernel(harmonic_ref, out_ref):
    row, col = iota((256, 256), 0), iota((256, 256), 1)
    interleave = one_hot(col == (row % 2) * 128 + row // 2)
    for i in range(8):
        out_ref[i] = dot(interleave, harmonic_ref[i], NT).astype(BF16)


def inverse_kernel(modes_ref, inv_ref, out_ref, sum_ref):
    total = modes_ref[0:256, :].astype(F32)
    for g in range(1, 8):
        total = total + modes_ref[g * 256 : (g + 1) * 256, :].astype(F32)
    sum_ref[...] = total
    blocks = []
    for q in range(4):
        parts = [sum_ref[pl.ds(c * 4 + q, 32, stride=8), :] for c in range(2)]
        turned = jnp.concatenate(parts, axis=0).T
        own = [turned[i * 16 : (i + 1) * 16, :] for i in range(8)]
        blocks.append(jnp.concatenate(own, axis=1))
    left = jnp.concatenate(blocks, axis=0).astype(BF16)
    result = dot(left, inv_ref[...])
    for q in range(4):
        out_ref[:, q, :] = result[q * 16 : (q + 1) * 16, :]


VMEM_SPEC = pl.BlockSpec(memory_space=pltpu.VMEM)
SMEM_SPEC = pl.BlockSpec(memory_space=pltpu.SMEM)
HBM_SPEC = pl.BlockSpec(memory_space=pltpu.HBM)


LIMIT = pltpu.CompilerParams(vmem_limit_bytes=24 << 20)


def on_chip(a):
    return pltpu.with_memory_space_constraint(a, pltpu.VMEM)


def off_chip(a):
    return pltpu.with_memory_space_constraint(a, pltpu.HBM)


def local(density, degree_weights, row_orders, target_cycles):
    forward_trig, inverse_trig = trig_tables(256, 512, 256)
    orders_row = row_orders.reshape(1, 256)
    own_orders = lax.dynamic_slice_in_dim(row_orders, lax.axis_index("ord") * 8, 8)
    centers = (jnp.arange(256, dtype=F32) + 0.5) * (math.pi / 256)
    grid = jnp.stack([jnp.cos(centers), jnp.sin(centers), math.pi / 256 * jnp.sin(centers)])

    spectra = pl.pallas_call(
        forward_kernel,
        out_shape=pltpu.HBM((32, 128, 128), BF16),
        in_specs=[HBM_SPEC] * 3,
        out_specs=HBM_SPEC,
        scratch_shapes=[
            pltpu.VMEM((1, 256), jnp.int32),
            pltpu.VMEM((1024, 512), BF16),
            pltpu.VMEM((256, 1024), BF16),
            pltpu.VMEM((8, 128, 512), BF16),
            pltpu.VMEM((32, 128, 128), BF16),
            pltpu.SemaphoreType.DMA(()),
            pltpu.SemaphoreType.DMA(()),
            pltpu.SemaphoreType.DMA((4,)),
            pltpu.SemaphoreType.DMA((4,)),
        ],
        name="forward",
        compiler_params=LIMIT,
    )(off_chip(orders_row), off_chip(density.reshape(1024, 512)), off_chip(jnp.asarray(forward_trig)))
    by_order = lax.all_to_all(spectra, "ord", split_axis=0, concat_axis=0, tiled=True)

    legendre, inverse_rows = pl.pallas_call(
        table_kernel,
        out_shape=(
            pltpu.VMEM((8, 384, 256), BF16),
            pltpu.HBM((512, 512), BF16),
        ),
        in_specs=[SMEM_SPEC] + [VMEM_SPEC] * 4,
        out_specs=(VMEM_SPEC,) * 2,
        scratch_shapes=[pltpu.VMEM((2, 2048, 128), F32), pltpu.VMEM((8, 256, 128), F32)],
        name="tables",
        compiler_params=LIMIT,
    )(own_orders, orders_row, target_cycles.reshape(1, 128), grid, jnp.asarray(inverse_trig))

    harmonic, modes = pl.pallas_call(
        order_kernel,
        out_shape=(pltpu.HBM((8, 256, 256), BF16), pltpu.HBM((2048, 128), BF16)),
        in_specs=[VMEM_SPEC] * 3,
        out_specs=(HBM_SPEC,) * 2,
        scratch_shapes=[
            pltpu.VMEM((16, 256, 128), BF16),
            pltpu.VMEM((8, 128, 256), BF16),
            pltpu.VMEM((8, 256, 256), BF16),
            pltpu.VMEM((2048, 128), BF16),
            pltpu.SemaphoreType.DMA((8,)),
            pltpu.SemaphoreType.DMA((8,)),
        ],
        name="orders",
        compiler_params=LIMIT,
    )(on_chip(by_order.reshape(4096, 128)), on_chip(legendre), degree_weights)

    arrived = lax.all_to_all(
        modes.reshape(256, 8, 128), ("band", "ord"), split_axis=0, concat_axis=0, tiled=True
    )
    coeffs = pl.pallas_call(
        coeffs_kernel,
        out_shape=pltpu.VMEM((8, 256, 256), BF16),
        in_specs=[VMEM_SPEC],
        out_specs=VMEM_SPEC,
        name="coeffs",
        compiler_params=LIMIT,
    )(harmonic)
    potential = pl.pallas_call(
        inverse_kernel,
        out_shape=jax.ShapeDtypeStruct((16, 4, 512), F32),
        in_specs=[VMEM_SPEC] * 2,
        out_specs=VMEM_SPEC,
        scratch_shapes=[pltpu.VMEM((256, 128), F32)],
        name="inverse",
        compiler_params=LIMIT,
    )(on_chip(arrived.reshape(2048, 128)), inverse_rows)
    return coeffs.reshape(1, 8, 128, 2, 256), potential


def solution(mesh):
    in_specs = (P("band", None, "ord", None), P("band", None), P(), P())
    out_specs = (P("band", "ord", None, None, None), P("band", "ord", None))
    return jax.shard_map(local, mesh=mesh, in_specs=in_specs, out_specs=out_specs, check_vma=False)
```

```python
import math

import numpy as np
import jax
import jax.numpy as jnp
from jax import lax
from jax.experimental import pallas as pl
from jax.experimental.pallas import tpu as pltpu
from jax.sharding import PartitionSpec as P

F32 = jnp.float32
BF16 = jnp.bfloat16
NN = (((1,), (0,)), ((), ()))
NT = (((1,), (1,)), ((), ()))
TN = (((0,), (0,)), ((), ()))


def dot(a, b, dims=NN):
    return lax.dot_general(a, b, dims, preferred_element_type=F32)


def trig_tables(order_count, lon_count, lat_count):
    turns = np.arange(order_count)[:, None] * np.arange(lon_count)[None, :] % lon_count
    phases = turns * (2.0 * math.pi / lon_count)
    gain = math.sqrt(lat_count * lon_count / (4.0 * math.pi))
    waves = np.concatenate([np.cos(phases), -np.sin(phases)], axis=1)
    forward = waves * (2.0 * math.pi / lon_count * gain)
    twice = np.where(np.arange(order_count) == 0, 1.0, 2.0)[:, None]
    inverse = waves * twice / gain
    kind = jnp.dtype(BF16)
    return forward.astype(np.float32).astype(kind), inverse.astype(np.float32).astype(kind)


def iota(shape, axis):
    return lax.broadcasted_iota(jnp.int32, shape, axis)


def one_hot(hit):
    return jnp.where(hit, 1.0, 0.0).astype(BF16)


def swap_matrix(outer, inner):
    n = outer * inner
    row, col = iota((n, n), 0), iota((n, n), 1)
    return one_hot(col == (row % inner) * outer + row // inner)


def forward_kernel(orders_hbm, density_hbm, table_hbm, out_hbm,
                   orders_ref, density_ref, table_ref, turned_ref, out_ref, in_sem, out_sem):
    orders_copy = pltpu.make_async_copy(orders_hbm, orders_ref, in_sem.at[0])
    table_copy = pltpu.make_async_copy(table_hbm, table_ref, in_sem.at[1])
    density_copy = pltpu.make_async_copy(density_hbm, density_ref, in_sem.at[2])
    orders_copy.start()
    table_copy.start()
    density_copy.start()
    swap = swap_matrix(8, 32)
    orders_copy.wait()
    hits = jnp.where(iota((256, 256), 0) == orders_ref[...], 1.0, 0.0)
    picks = hits.T.astype(BF16)
    table_copy.wait()
    rows = dot(picks, table_ref[...])
    cos_rows = rows[:, :512].reshape(32, 8, 512)
    sin_rows = rows[:, 512:].reshape(32, 8, 512)
    forward = jnp.stack([cos_rows, sin_rows], axis=1).reshape(512, 512).astype(BF16)
    density_copy.wait()
    for b in range(4):
        part = dot(swap, density_ref[b * 256 : (b + 1) * 256, :]).astype(BF16)
        turned_ref[:, b * 32 : (b + 1) * 32, :] = part.reshape(8, 32, 512)
    sends = []
    for j in range(0, 8, 2):
        lanes = turned_ref[j : j + 2].reshape(256, 512)
        part = dot(forward, lanes, NT).astype(BF16)
        for h in range(2):
            block = part[:, h * 128 : (h + 1) * 128].reshape(32, 16, 128)
            out_ref[:, (j + h) * 16 : (j + h + 1) * 16, :] = block
        if j in (2, 6):
            half = pl.ds((j - 2) * 16, 64)
            send = pltpu.make_async_copy(out_ref.at[:, half], out_hbm.at[:, half], out_sem.at[j // 4])
            send.start()
            sends.append(send)
    for send in sends:
        send.wait()


def table_kernel(own_ref, orders_ref, target_ref, grid_ref, inverse_ref,
                 legendre_out_ref, inv_ref, legendre_ref, rows_ref):
    sub = iota((8, 256), 0)
    order = jnp.zeros((8, 256), F32)
    for i in range(8):
        order = jnp.where(sub == i, own_ref[i].astype(F32), order)
    cosines = jnp.broadcast_to(grid_ref[0:1, :], (8, 256))
    log_sines = jnp.log(grid_ref[1:2, :])
    weights = grid_ref[2:3, :]
    steps = iota((8, 256), 1).astype(F32)
    safe = jnp.maximum(steps, 1.0)
    log_terms = jnp.log((2.0 * safe + 1.0) / (2.0 * safe))
    counted = (steps >= 1.0) & (steps <= order)
    gamma = jnp.sum(jnp.where(counted, log_terms, 0.0), axis=1, keepdims=True)
    log_start = 0.5 * (math.log(1.0 / (4.0 * math.pi)) + gamma) + order * log_sines
    shift = jnp.clip(-log_start - 40.0, 0.0, 80.0)
    sectoral = jnp.exp(log_start + shift)
    unshift = jnp.exp(-shift)
    half = order[:, :128]
    half_sq = half * half

    def wide(a):
        return jnp.concatenate([a, a], axis=1)

    def advance(step, carry):
        previous, earlier = carry
        degree = jnp.full((8, 128), step, jnp.int32).astype(F32)
        square = degree * degree
        growth = jnp.sqrt(
            jnp.maximum(4.0 * square - 1.0, 0.0) / jnp.maximum(square - half_sq, 1.0)
        )
        lower = degree - 1.0
        low_sq = lower * lower
        damping = jnp.sqrt(
            jnp.maximum(low_sq - half_sq, 0.0) / jnp.maximum(4.0 * low_sq - 1.0, 1.0)
        )
        grown = wide(growth) * (cosines * previous - wide(damping) * earlier)
        wide_degree = wide(degree)
        current = jnp.where(
            wide_degree < order, 0.0, jnp.where(wide_degree == order, sectoral, grown)
        )
        final = current * unshift
        rows = pl.ds(pl.multiple_of(step * 8, 8), 8)
        legendre_ref[0, rows, :] = final[:, :128]
        legendre_ref[1, rows, :] = final[:, 128:]
        return current, previous

    empty = sectoral * 0.0
    lax.fori_loop(0, 256, advance, (empty, empty), unroll=8)

    hits = jnp.where(iota((256, 128), 0) == target_ref[...], 1.0, 0.0)
    picks = hits.T.astype(BF16)
    for i in range(8):
        halves = [legendre_ref[h, pl.ds(i, 256, stride=8), :] for h in range(2)]
        own = jnp.concatenate(halves, axis=1)
        legendre_out_ref[i, :256, :] = (own * weights).astype(BF16)
        legendre_out_ref[i, 256:, :] = dot(picks, own.astype(BF16), NT).astype(BF16)

    places = one_hot(iota((256, 256), 0) == orders_ref[...])
    rows = dot(places, inverse_ref[...], TN)
    for c in range(8):
        rows_ref[c] = rows[:, c * 128 : (c + 1) * 128]
    for i in range(8):
        for c in range(8):
            own = rows_ref[c, pl.ds(i, 32, stride=8), :].astype(BF16)
            top = i * 64 + c // 4 * 32
            inv_ref[top : top + 32, c % 4 * 128 : (c % 4 + 1) * 128] = own


def order_kernel(spectra_ref, legendre_ref, weights_ref,
                 harmonic_hbm, out_hbm, cycles_ref, modes_ref, harmonic_ref, out_ref, out_sem):
    swap = swap_matrix(16, 16)
    for b in range(0, 16, 2):
        first = spectra_ref[b * 256 : (b + 1) * 256, :]
        second = spectra_ref[(b + 1) * 256 : (b + 2) * 256, :]
        both = dot(swap, jnp.concatenate([first, second], axis=1)).astype(BF16)
        cycles_ref[:, b * 16 : (b + 1) * 16, :] = both[:, :128].reshape(16, 16, 128)
        cycles_ref[:, (b + 1) * 16 : (b + 2) * 16, :] = both[:, 128:].reshape(16, 16, 128)
    scale = jnp.broadcast_to(weights_ref[...], (128, 256)).T
    scale = jnp.concatenate([scale, scale], axis=1)
    row, col = iota((256, 256), 0), iota((256, 256), 1)
    deal = one_hot(col == (row // 4 % 2) * 128 + row // 8 * 4 + row % 4)
    for i in range(8):
        lanes = jnp.concatenate([cycles_ref[i], cycles_ref[8 + i]], axis=1)
        harmonic_ref[i] = dot(legendre_ref[i, :256, :], lanes).astype(BF16)
    for i in range(8):
        scaled = (harmonic_ref[i].astype(F32) * scale).astype(BF16)
        modes = dot(legendre_ref[i, 256:, :], scaled).astype(BF16)
        modes_ref[:, i * 16 : (i + 1) * 16, :] = modes.reshape(8, 16, 256)
    sends = [pltpu.make_async_copy(harmonic_ref, harmonic_hbm, out_sem.at[2])]
    sends[0].start()
    for b in range(0, 8, 2):
        pair = modes_ref[b : b + 2].reshape(256, 256)
        block = dot(deal, pair, NT).astype(BF16)
        out_ref[b * 256 : (b + 1) * 256, :] = block[:, :128]
        out_ref[(b + 1) * 256 : (b + 2) * 256, :] = block[:, 128:]
        if b in (2, 6):
            half = pl.ds((b - 2) * 256, 1024)
            send = pltpu.make_async_copy(out_ref.at[half], out_hbm.at[half], out_sem.at[b // 4])
            send.start()
            sends.append(send)
    for send in sends:
        send.wait()


def coeffs_kernel(harmonic_ref, out_ref):
    row, col = iota((256, 256), 0), iota((256, 256), 1)
    interleave = one_hot(col == (row % 2) * 128 + row // 2)
    for i in range(8):
        out_ref[i] = dot(interleave, harmonic_ref[i], NT).astype(BF16)


def inverse_kernel(modes_ref, inv_ref, out_ref, sum_ref):
    total = modes_ref[0:256, :].astype(F32)
    for g in range(1, 8):
        total = total + modes_ref[g * 256 : (g + 1) * 256, :].astype(F32)
    sum_ref[...] = total
    blocks = []
    for q in range(4):
        parts = [sum_ref[pl.ds(c * 4 + q, 32, stride=8), :] for c in range(2)]
        turned = jnp.concatenate(parts, axis=0).T
        own = [turned[i * 16 : (i + 1) * 16, :] for i in range(8)]
        blocks.append(jnp.concatenate(own, axis=1))
    left = jnp.concatenate(blocks, axis=0).astype(BF16)
    result = dot(left, inv_ref[...])
    for q in range(4):
        out_ref[:, q, :] = result[q * 16 : (q + 1) * 16, :]


VMEM_SPEC = pl.BlockSpec(memory_space=pltpu.VMEM)
SMEM_SPEC = pl.BlockSpec(memory_space=pltpu.SMEM)
HBM_SPEC = pl.BlockSpec(memory_space=pltpu.HBM)


LIMIT = pltpu.CompilerParams(vmem_limit_bytes=24 << 20)


def on_chip(a):
    return pltpu.with_memory_space_constraint(a, pltpu.VMEM)


def off_chip(a):
    return pltpu.with_memory_space_constraint(a, pltpu.HBM)


def local(density, degree_weights, row_orders, target_cycles):
    forward_trig, inverse_trig = trig_tables(256, 512, 256)
    orders_row = row_orders.reshape(1, 256)
    own_orders = lax.dynamic_slice_in_dim(row_orders, lax.axis_index("ord") * 8, 8)
    centers = (jnp.arange(256, dtype=F32) + 0.5) * (math.pi / 256)
    grid = jnp.stack([jnp.cos(centers), jnp.sin(centers), math.pi / 256 * jnp.sin(centers)])

    spectra = pl.pallas_call(
        forward_kernel,
        out_shape=pltpu.HBM((32, 128, 128), BF16),
        in_specs=[HBM_SPEC] * 3,
        out_specs=HBM_SPEC,
        scratch_shapes=[
            pltpu.VMEM((1, 256), jnp.int32),
            pltpu.VMEM((1024, 512), BF16),
            pltpu.VMEM((256, 1024), BF16),
            pltpu.VMEM((8, 128, 512), BF16),
            pltpu.VMEM((32, 128, 128), BF16),
            pltpu.SemaphoreType.DMA((3,)),
            pltpu.SemaphoreType.DMA((2,)),
        ],
        name="forward",
        compiler_params=LIMIT,
    )(off_chip(orders_row), off_chip(density.reshape(1024, 512)), off_chip(jnp.asarray(forward_trig)))
    by_order = lax.all_to_all(spectra, "ord", split_axis=0, concat_axis=0, tiled=True)

    legendre, inverse_rows = pl.pallas_call(
        table_kernel,
        out_shape=(
            pltpu.VMEM((8, 384, 256), BF16),
            pltpu.HBM((512, 512), BF16),
        ),
        in_specs=[SMEM_SPEC] + [VMEM_SPEC] * 4,
        out_specs=(VMEM_SPEC,) * 2,
        scratch_shapes=[pltpu.VMEM((2, 2048, 128), F32), pltpu.VMEM((8, 256, 128), F32)],
        name="tables",
        compiler_params=LIMIT,
    )(own_orders, orders_row, target_cycles.reshape(1, 128), grid, jnp.asarray(inverse_trig))

    harmonic, modes = pl.pallas_call(
        order_kernel,
        out_shape=(pltpu.HBM((8, 256, 256), BF16), pltpu.HBM((2048, 128), BF16)),
        in_specs=[VMEM_SPEC] * 3,
        out_specs=(HBM_SPEC,) * 2,
        scratch_shapes=[
            pltpu.VMEM((16, 256, 128), BF16),
            pltpu.VMEM((8, 128, 256), BF16),
            pltpu.VMEM((8, 256, 256), BF16),
            pltpu.VMEM((2048, 128), BF16),
            pltpu.SemaphoreType.DMA((3,)),
        ],
        name="orders",
        compiler_params=LIMIT,
    )(on_chip(by_order.reshape(4096, 128)), on_chip(legendre), degree_weights)

    arrived = lax.all_to_all(
        modes.reshape(256, 8, 128), ("band", "ord"), split_axis=0, concat_axis=0, tiled=True
    )
    coeffs = pl.pallas_call(
        coeffs_kernel,
        out_shape=pltpu.VMEM((8, 256, 256), BF16),
        in_specs=[VMEM_SPEC],
        out_specs=VMEM_SPEC,
        name="coeffs",
        compiler_params=LIMIT,
    )(harmonic)
    potential = pl.pallas_call(
        inverse_kernel,
        out_shape=jax.ShapeDtypeStruct((16, 4, 512), F32),
        in_specs=[VMEM_SPEC] * 2,
        out_specs=VMEM_SPEC,
        scratch_shapes=[pltpu.VMEM((256, 128), F32)],
        name="inverse",
        compiler_params=LIMIT,
    )(on_chip(arrived.reshape(2048, 128)), inverse_rows)
    return coeffs.reshape(1, 8, 128, 2, 256), potential


def solution(mesh):
    in_specs = (P("band", None, "ord", None), P("band", None), P(), P())
    out_specs = (P("band", "ord", None, None, None), P("band", "ord", None))
    return jax.shard_map(local, mesh=mesh, in_specs=in_specs, out_specs=out_specs, check_vma=False)
```

```python
import math

import numpy as np
import jax
import jax.numpy as jnp
from jax import lax
from jax.experimental import pallas as pl
from jax.experimental.pallas import tpu as pltpu
from jax.sharding import PartitionSpec as P

F32 = jnp.float32
BF16 = jnp.bfloat16
NN = (((1,), (0,)), ((), ()))
NT = (((1,), (1,)), ((), ()))
TN = (((0,), (0,)), ((), ()))


def dot(a, b, dims=NN):
    return lax.dot_general(a, b, dims, preferred_element_type=F32)


def trig_tables(order_count, lon_count, lat_count):
    turns = np.arange(order_count)[:, None] * np.arange(lon_count)[None, :] % lon_count
    phases = turns * (2.0 * math.pi / lon_count)
    gain = math.sqrt(lat_count * lon_count / (4.0 * math.pi))
    waves = np.concatenate([np.cos(phases), -np.sin(phases)], axis=1)
    forward = waves * (2.0 * math.pi / lon_count * gain)
    twice = np.where(np.arange(order_count) == 0, 1.0, 2.0)[:, None]
    inverse = waves * twice / gain
    kind = jnp.dtype(BF16)
    return forward.astype(np.float32).astype(kind), inverse.astype(np.float32).astype(kind)


def iota(shape, axis):
    return lax.broadcasted_iota(jnp.int32, shape, axis)


def one_hot(hit):
    return jnp.where(hit, 1.0, 0.0).astype(BF16)


def swap_matrix(outer, inner):
    n = outer * inner
    row, col = iota((n, n), 0), iota((n, n), 1)
    return one_hot(col == (row % inner) * outer + row // inner)


def forward_kernel(orders_hbm, density_hbm, table_hbm, out_hbm,
                   orders_ref, density_ref, table_ref, turned_ref, out_ref, in_sem, out_sem):
    orders_copy = pltpu.make_async_copy(orders_hbm, orders_ref, in_sem.at[0])
    table_copy = pltpu.make_async_copy(table_hbm, table_ref, in_sem.at[1])
    density_copy = pltpu.make_async_copy(density_hbm, density_ref, in_sem.at[2])
    orders_copy.start()
    table_copy.start()
    density_copy.start()
    swap = swap_matrix(8, 32)
    orders_copy.wait()
    hits = jnp.where(iota((256, 256), 0) == orders_ref[...], 1.0, 0.0)
    picks = hits.T.astype(BF16)
    table_copy.wait()
    rows = dot(picks, table_ref[...])
    cos_rows = rows[:, :512].reshape(32, 8, 512)
    sin_rows = rows[:, 512:].reshape(32, 8, 512)
    forward = jnp.stack([cos_rows, sin_rows], axis=1).reshape(512, 512).astype(BF16)
    density_copy.wait()
    for b in range(4):
        part = dot(swap, density_ref[b * 256 : (b + 1) * 256, :]).astype(BF16)
        turned_ref[:, b * 32 : (b + 1) * 32, :] = part.reshape(8, 32, 512)
    sends = []
    for j in range(0, 8, 2):
        lanes = turned_ref[j : j + 2].reshape(256, 512)
        part = dot(forward, lanes, NT).astype(BF16)
        for h in range(2):
            block = part[:, h * 128 : (h + 1) * 128].reshape(32, 16, 128)
            out_ref[:, (j + h) * 16 : (j + h + 1) * 16, :] = block
        if j in (2, 6):
            half = pl.ds((j - 2) * 16, 64)
            send = pltpu.make_async_copy(out_ref.at[:, half], out_hbm.at[:, half], out_sem.at[j // 4])
            send.start()
            sends.append(send)
    for send in sends:
        send.wait()


def table_kernel(own_ref, orders_ref, target_ref, grid_ref, inverse_ref, weights_ref,
                 analysis_ref, transfer_ref, inv_ref, legendre_ref, rows_ref):
    sub = iota((8, 256), 0)
    order = jnp.zeros((8, 256), F32)
    for i in range(8):
        order = jnp.where(sub == i, own_ref[i].astype(F32), order)
    cosines = jnp.broadcast_to(grid_ref[0:1, :], (8, 256))
    log_sines = jnp.log(grid_ref[1:2, :])
    weights = grid_ref[2:3, :]
    steps = iota((8, 256), 1).astype(F32)
    safe = jnp.maximum(steps, 1.0)
    log_terms = jnp.log((2.0 * safe + 1.0) / (2.0 * safe))
    counted = (steps >= 1.0) & (steps <= order)
    gamma = jnp.sum(jnp.where(counted, log_terms, 0.0), axis=1, keepdims=True)
    log_start = 0.5 * (math.log(1.0 / (4.0 * math.pi)) + gamma) + order * log_sines
    shift = jnp.clip(-log_start - 40.0, 0.0, 80.0)
    sectoral = jnp.exp(log_start + shift)
    unshift = jnp.exp(-shift)
    half = order[:, :128]
    half_sq = half * half

    def wide(a):
        return jnp.concatenate([a, a], axis=1)

    def advance(step, carry):
        previous, earlier = carry
        degree = jnp.full((8, 128), step, jnp.int32).astype(F32)
        square = degree * degree
        growth = jnp.sqrt(
            jnp.maximum(4.0 * square - 1.0, 0.0) / jnp.maximum(square - half_sq, 1.0)
        )
        lower = degree - 1.0
        low_sq = lower * lower
        damping = jnp.sqrt(
            jnp.maximum(low_sq - half_sq, 0.0) / jnp.maximum(4.0 * low_sq - 1.0, 1.0)
        )
        grown = wide(growth) * (cosines * previous - wide(damping) * earlier)
        wide_degree = wide(degree)
        current = jnp.where(
            wide_degree < order, 0.0, jnp.where(wide_degree == order, sectoral, grown)
        )
        final = current * unshift
        rows = pl.ds(pl.multiple_of(step * 8, 8), 8)
        legendre_ref[0, rows, :] = final[:, :128]
        legendre_ref[1, rows, :] = final[:, 128:]
        return current, previous

    empty = sectoral * 0.0
    lax.fori_loop(0, 256, advance, (empty, empty), unroll=8)

    hits = jnp.where(iota((256, 128), 0) == target_ref[...], 1.0, 0.0)
    picks = hits.T.astype(BF16)
    for i in range(8):
        halves = [legendre_ref[h, pl.ds(i, 256, stride=8), :] for h in range(2)]
        own = jnp.concatenate(halves, axis=1)
        analysis = (own * weights).astype(BF16)
        synthesis = dot(picks, own.astype(BF16), NT)
        scaled = (synthesis * weights_ref[...]).astype(BF16)
        analysis_ref[i] = analysis
        transfer_ref[i] = dot(scaled, analysis).astype(BF16)

    places = one_hot(iota((256, 256), 0) == orders_ref[...])
    rows = dot(places, inverse_ref[...], TN)
    for c in range(8):
        rows_ref[c] = rows[:, c * 128 : (c + 1) * 128]
    for i in range(8):
        for c in range(8):
            own = rows_ref[c, pl.ds(i, 32, stride=8), :].astype(BF16)
            top = i * 64 + c // 4 * 32
            inv_ref[top : top + 32, c % 4 * 128 : (c % 4 + 1) * 128] = own


def turn_cycles(spectra_ref, cycles_ref):
    swap = swap_matrix(16, 16)
    for b in range(0, 16, 2):
        first = spectra_ref[b * 256 : (b + 1) * 256, :]
        second = spectra_ref[(b + 1) * 256 : (b + 2) * 256, :]
        both = dot(swap, jnp.concatenate([first, second], axis=1)).astype(BF16)
        cycles_ref[:, b * 16 : (b + 1) * 16, :] = both[:, :128].reshape(16, 16, 128)
        cycles_ref[:, (b + 1) * 16 : (b + 2) * 16, :] = both[:, 128:].reshape(16, 16, 128)


def mode_kernel(spectra_ref, transfer_ref, out_hbm, cycles_ref, modes_ref, out_ref, out_sem):
    turn_cycles(spectra_ref, cycles_ref)
    row, col = iota((256, 256), 0), iota((256, 256), 1)
    deal = one_hot(col == (row // 4 % 2) * 128 + row // 8 * 4 + row % 4)
    for i in range(8):
        lanes = jnp.concatenate([cycles_ref[i], cycles_ref[8 + i]], axis=1)
        modes = dot(transfer_ref[i], lanes).astype(BF16)
        modes_ref[:, i * 16 : (i + 1) * 16, :] = modes.reshape(8, 16, 256)
    sends = []
    for b in range(0, 8, 2):
        pair = modes_ref[b : b + 2].reshape(256, 256)
        block = dot(deal, pair, NT).astype(BF16)
        out_ref[b * 256 : (b + 1) * 256, :] = block[:, :128]
        out_ref[(b + 1) * 256 : (b + 2) * 256, :] = block[:, 128:]
        if b in (2, 6):
            half = pl.ds((b - 2) * 256, 1024)
            send = pltpu.make_async_copy(out_ref.at[half], out_hbm.at[half], out_sem.at[b // 4])
            send.start()
            sends.append(send)
    for send in sends:
        send.wait()


def coeffs_kernel(spectra_ref, analysis_ref, out_ref, cycles_ref):
    turn_cycles(spectra_ref, cycles_ref)
    row, col = iota((256, 256), 0), iota((256, 256), 1)
    interleave = one_hot(col == (row % 2) * 128 + row // 2)
    for i in range(8):
        lanes = jnp.concatenate([cycles_ref[i], cycles_ref[8 + i]], axis=1)
        harmonic = dot(analysis_ref[i], lanes).astype(BF16)
        out_ref[i] = dot(interleave, harmonic, NT).astype(BF16)


def inverse_kernel(modes_ref, inv_ref, out_ref, sum_ref):
    total = modes_ref[0:256, :].astype(F32)
    for g in range(1, 8):
        total = total + modes_ref[g * 256 : (g + 1) * 256, :].astype(F32)
    sum_ref[...] = total
    blocks = []
    for q in range(4):
        parts = [sum_ref[pl.ds(c * 4 + q, 32, stride=8), :] for c in range(2)]
        turned = jnp.concatenate(parts, axis=0).T
        own = [turned[i * 16 : (i + 1) * 16, :] for i in range(8)]
        blocks.append(jnp.concatenate(own, axis=1))
    left = jnp.concatenate(blocks, axis=0).astype(BF16)
    result = dot(left, inv_ref[...])
    for q in range(4):
        out_ref[:, q, :] = result[q * 16 : (q + 1) * 16, :]


VMEM_SPEC = pl.BlockSpec(memory_space=pltpu.VMEM)
SMEM_SPEC = pl.BlockSpec(memory_space=pltpu.SMEM)
HBM_SPEC = pl.BlockSpec(memory_space=pltpu.HBM)


LIMIT = pltpu.CompilerParams(vmem_limit_bytes=24 << 20)


def on_chip(a):
    return pltpu.with_memory_space_constraint(a, pltpu.VMEM)


def off_chip(a):
    return pltpu.with_memory_space_constraint(a, pltpu.HBM)


def local(density, degree_weights, row_orders, target_cycles):
    forward_trig, inverse_trig = trig_tables(256, 512, 256)
    orders_row = row_orders.reshape(1, 256)
    own_orders = lax.dynamic_slice_in_dim(row_orders, lax.axis_index("ord") * 8, 8)
    centers = (jnp.arange(256, dtype=F32) + 0.5) * (math.pi / 256)
    grid = jnp.stack([jnp.cos(centers), jnp.sin(centers), math.pi / 256 * jnp.sin(centers)])

    spectra = pl.pallas_call(
        forward_kernel,
        out_shape=pltpu.HBM((32, 128, 128), BF16),
        in_specs=[HBM_SPEC] * 3,
        out_specs=HBM_SPEC,
        scratch_shapes=[
            pltpu.VMEM((1, 256), jnp.int32),
            pltpu.VMEM((1024, 512), BF16),
            pltpu.VMEM((256, 1024), BF16),
            pltpu.VMEM((8, 128, 512), BF16),
            pltpu.VMEM((32, 128, 128), BF16),
            pltpu.SemaphoreType.DMA((3,)),
            pltpu.SemaphoreType.DMA((2,)),
        ],
        name="forward",
        compiler_params=LIMIT,
    )(off_chip(orders_row), off_chip(density.reshape(1024, 512)), off_chip(jnp.asarray(forward_trig)))
    by_order = lax.all_to_all(spectra, "ord", split_axis=0, concat_axis=0, tiled=True)

    analysis, transfer, inverse_rows = pl.pallas_call(
        table_kernel,
        out_shape=(
            pltpu.HBM((8, 256, 256), BF16),
            pltpu.VMEM((8, 128, 256), BF16),
            pltpu.HBM((512, 512), BF16),
        ),
        in_specs=[SMEM_SPEC] + [VMEM_SPEC] * 5,
        out_specs=(VMEM_SPEC,) * 3,
        scratch_shapes=[pltpu.VMEM((2, 2048, 128), F32), pltpu.VMEM((8, 256, 128), F32)],
        name="tables",
        compiler_params=LIMIT,
    )(own_orders, orders_row, target_cycles.reshape(1, 128), grid, jnp.asarray(inverse_trig),
      degree_weights)

    received = on_chip(by_order.reshape(4096, 128))
    modes = pl.pallas_call(
        mode_kernel,
        out_shape=pltpu.HBM((2048, 128), BF16),
        in_specs=[VMEM_SPEC] * 2,
        out_specs=HBM_SPEC,
        scratch_shapes=[
            pltpu.VMEM((16, 256, 128), BF16),
            pltpu.VMEM((8, 128, 256), BF16),
            pltpu.VMEM((2048, 128), BF16),
            pltpu.SemaphoreType.DMA((2,)),
        ],
        name="modes",
        compiler_params=LIMIT,
    )(received, on_chip(transfer))

    arrived = lax.all_to_all(
        modes.reshape(256, 8, 128), ("band", "ord"), split_axis=0, concat_axis=0, tiled=True
    )
    coeffs = pl.pallas_call(
        coeffs_kernel,
        out_shape=pltpu.VMEM((8, 256, 256), BF16),
        in_specs=[VMEM_SPEC] * 2,
        out_specs=VMEM_SPEC,
        scratch_shapes=[pltpu.VMEM((16, 256, 128), BF16)],
        name="coeffs",
        compiler_params=LIMIT,
    )(received, analysis)
    potential = pl.pallas_call(
        inverse_kernel,
        out_shape=jax.ShapeDtypeStruct((16, 4, 512), F32),
        in_specs=[VMEM_SPEC] * 2,
        out_specs=VMEM_SPEC,
        scratch_shapes=[pltpu.VMEM((256, 128), F32)],
        name="inverse",
        compiler_params=LIMIT,
    )(on_chip(arrived.reshape(2048, 128)), inverse_rows)
    return coeffs.reshape(1, 8, 128, 2, 256), potential


def solution(mesh):
    in_specs = (P("band", None, "ord", None), P("band", None), P(), P())
    out_specs = (P("band", "ord", None, None, None), P("band", "ord", None))
    return jax.shard_map(local, mesh=mesh, in_specs=in_specs, out_specs=out_specs, check_vma=False)
```

```python
import math

import numpy as np
import jax
import jax.numpy as jnp
from jax import lax
from jax.experimental import pallas as pl
from jax.experimental.pallas import tpu as pltpu
from jax.sharding import PartitionSpec as P

F32 = jnp.float32
BF16 = jnp.bfloat16
NN = (((1,), (0,)), ((), ()))
NT = (((1,), (1,)), ((), ()))
TN = (((0,), (0,)), ((), ()))


def dot(a, b, dims=NN):
    return lax.dot_general(a, b, dims, preferred_element_type=F32)


def trig_tables(order_count, lon_count, lat_count):
    turns = np.arange(order_count)[:, None] * np.arange(lon_count)[None, :] % lon_count
    phases = turns * (2.0 * math.pi / lon_count)
    gain = math.sqrt(lat_count * lon_count / (4.0 * math.pi))
    waves = np.concatenate([np.cos(phases), -np.sin(phases)], axis=1)
    forward = waves * (2.0 * math.pi / lon_count * gain)
    twice = np.where(np.arange(order_count) == 0, 1.0, 2.0)[:, None]
    inverse = waves * twice / gain
    kind = jnp.dtype(BF16)
    return forward.astype(np.float32).astype(kind), inverse.astype(np.float32).astype(kind)


def iota(shape, axis):
    return lax.broadcasted_iota(jnp.int32, shape, axis)


def one_hot(hit):
    return jnp.where(hit, 1.0, 0.0).astype(BF16)


def split(a):
    high = a.astype(BF16)
    return high, (a - high.astype(F32)).astype(BF16)


def swap_matrix(outer, inner):
    n = outer * inner
    row, col = iota((n, n), 0), iota((n, n), 1)
    return one_hot(col == (row % inner) * outer + row // inner)


def forward_kernel(orders_hbm, density_hbm, table_hbm, out_hbm,
                   orders_ref, density_ref, table_ref, turned_ref, out_ref, in_sem, out_sem):
    orders_copy = pltpu.make_async_copy(orders_hbm, orders_ref, in_sem.at[0])
    table_copy = pltpu.make_async_copy(table_hbm, table_ref, in_sem.at[1])
    density_copy = pltpu.make_async_copy(density_hbm, density_ref, in_sem.at[2])
    orders_copy.start()
    table_copy.start()
    density_copy.start()
    swap = swap_matrix(8, 32)
    orders_copy.wait()
    hits = jnp.where(iota((256, 256), 0) == orders_ref[...], 1.0, 0.0)
    picks = hits.T.astype(BF16)
    table_copy.wait()
    rows = dot(picks, table_ref[...])
    cos_rows = rows[:, :512].reshape(32, 8, 512)
    sin_rows = rows[:, 512:].reshape(32, 8, 512)
    forward = jnp.stack([cos_rows, sin_rows], axis=1).reshape(512, 512).astype(BF16)
    density_copy.wait()
    for b in range(4):
        part = dot(swap, density_ref[b * 256 : (b + 1) * 256, :]).astype(BF16)
        turned_ref[:, b * 32 : (b + 1) * 32, :] = part.reshape(8, 32, 512)
    sends = []
    for j in range(0, 8, 2):
        lanes = turned_ref[j : j + 2].reshape(256, 512)
        part = dot(forward, lanes, NT).astype(BF16)
        for h in range(2):
            block = part[:, h * 128 : (h + 1) * 128].reshape(32, 16, 128)
            out_ref[:, (j + h) * 16 : (j + h + 1) * 16, :] = block
        if j in (2, 6):
            half = pl.ds((j - 2) * 16, 64)
            send = pltpu.make_async_copy(out_ref.at[:, half], out_hbm.at[:, half], out_sem.at[j // 4])
            send.start()
            sends.append(send)
    for send in sends:
        send.wait()


def table_kernel(own_ref, orders_ref, target_ref, grid_ref, inverse_ref, weights_ref,
                 analysis_ref, transfer_ref, inv_ref, legendre_ref, rows_ref):
    sub = iota((8, 256), 0)
    order = jnp.zeros((8, 256), F32)
    for i in range(8):
        order = jnp.where(sub == i, own_ref[i].astype(F32), order)
    cosines = jnp.broadcast_to(grid_ref[0:1, :], (8, 256))
    log_sines = jnp.log(grid_ref[1:2, :])
    weights = grid_ref[2:3, :]
    steps = iota((8, 256), 1).astype(F32)
    safe = jnp.maximum(steps, 1.0)
    log_terms = jnp.log((2.0 * safe + 1.0) / (2.0 * safe))
    counted = (steps >= 1.0) & (steps <= order)
    gamma = jnp.sum(jnp.where(counted, log_terms, 0.0), axis=1, keepdims=True)
    log_start = 0.5 * (math.log(1.0 / (4.0 * math.pi)) + gamma) + order * log_sines
    shift = jnp.clip(-log_start - 40.0, 0.0, 80.0)
    sectoral = jnp.exp(log_start + shift)
    unshift = jnp.exp(-shift)
    half = order[:, :128]
    half_sq = half * half

    def wide(a):
        return jnp.concatenate([a, a], axis=1)

    def advance(step, carry):
        previous, earlier = carry
        degree = jnp.full((8, 128), step, jnp.int32).astype(F32)
        square = degree * degree
        growth = jnp.sqrt(
            jnp.maximum(4.0 * square - 1.0, 0.0) / jnp.maximum(square - half_sq, 1.0)
        )
        lower = degree - 1.0
        low_sq = lower * lower
        damping = jnp.sqrt(
            jnp.maximum(low_sq - half_sq, 0.0) / jnp.maximum(4.0 * low_sq - 1.0, 1.0)
        )
        grown = wide(growth) * (cosines * previous - wide(damping) * earlier)
        wide_degree = wide(degree)
        current = jnp.where(
            wide_degree < order, 0.0, jnp.where(wide_degree == order, sectoral, grown)
        )
        final = current * unshift
        rows = pl.ds(pl.multiple_of(step * 8, 8), 8)
        legendre_ref[0, rows, :] = final[:, :128]
        legendre_ref[1, rows, :] = final[:, 128:]
        return current, previous

    empty = sectoral * 0.0
    lax.fori_loop(0, 256, advance, (empty, empty), unroll=8)

    hits = jnp.where(iota((256, 128), 0) == target_ref[...], 1.0, 0.0)
    picks = hits.T.astype(BF16)
    for i in range(8):
        halves = [legendre_ref[h, pl.ds(i, 256, stride=8), :] for h in range(2)]
        own = jnp.concatenate(halves, axis=1)
        analysis = (own * weights).astype(BF16)
        synthesis = dot(picks, own.astype(BF16), NT)
        high, low = split(synthesis * weights_ref[...])
        analysis_ref[i] = analysis
        transfer_ref[i] = (dot(high, analysis) + dot(low, analysis)).astype(BF16)

    places = one_hot(iota((256, 256), 0) == orders_ref[...])
    rows = dot(places, inverse_ref[...], TN)
    for c in range(8):
        rows_ref[c] = rows[:, c * 128 : (c + 1) * 128]
    for i in range(8):
        for c in range(8):
            own = rows_ref[c, pl.ds(i, 32, stride=8), :].astype(BF16)
            top = i * 64 + c // 4 * 32
            inv_ref[top : top + 32, c % 4 * 128 : (c % 4 + 1) * 128] = own


def turn_cycles(spectra_ref, cycles_ref):
    swap = swap_matrix(16, 16)
    for b in range(0, 16, 2):
        first = spectra_ref[b * 256 : (b + 1) * 256, :]
        second = spectra_ref[(b + 1) * 256 : (b + 2) * 256, :]
        both = dot(swap, jnp.concatenate([first, second], axis=1)).astype(BF16)
        cycles_ref[:, b * 16 : (b + 1) * 16, :] = both[:, :128].reshape(16, 16, 128)
        cycles_ref[:, (b + 1) * 16 : (b + 2) * 16, :] = both[:, 128:].reshape(16, 16, 128)


def mode_kernel(spectra_ref, transfer_ref, out_hbm, cycles_ref, modes_ref, out_ref, out_sem):
    turn_cycles(spectra_ref, cycles_ref)
    row, col = iota((256, 256), 0), iota((256, 256), 1)
    deal = one_hot(col == (row // 4 % 2) * 128 + row // 8 * 4 + row % 4)
    for i in range(8):
        lanes = jnp.concatenate([cycles_ref[i], cycles_ref[8 + i]], axis=1)
        modes = dot(transfer_ref[i], lanes).astype(BF16)
        modes_ref[:, i * 16 : (i + 1) * 16, :] = modes.reshape(8, 16, 256)
    sends = []
    for b in range(0, 8, 2):
        pair = modes_ref[b : b + 2].reshape(256, 256)
        block = dot(deal, pair, NT).astype(BF16)
        out_ref[b * 256 : (b + 1) * 256, :] = block[:, :128]
        out_ref[(b + 1) * 256 : (b + 2) * 256, :] = block[:, 128:]
        if b in (2, 6):
            half = pl.ds((b - 2) * 256, 1024)
            send = pltpu.make_async_copy(out_ref.at[half], out_hbm.at[half], out_sem.at[b // 4])
            send.start()
            sends.append(send)
    for send in sends:
        send.wait()


def coeffs_kernel(spectra_ref, analysis_ref, out_ref, cycles_ref):
    turn_cycles(spectra_ref, cycles_ref)
    row, col = iota((256, 256), 0), iota((256, 256), 1)
    interleave = one_hot(col == (row % 2) * 128 + row // 2)
    for i in range(8):
        lanes = jnp.concatenate([cycles_ref[i], cycles_ref[8 + i]], axis=1)
        harmonic = dot(analysis_ref[i], lanes).astype(BF16)
        out_ref[i] = dot(interleave, harmonic, NT).astype(BF16)


def inverse_kernel(modes_ref, inv_ref, out_ref, sum_ref):
    total = modes_ref[0:256, :].astype(F32)
    for g in range(1, 8):
        total = total + modes_ref[g * 256 : (g + 1) * 256, :].astype(F32)
    sum_ref[...] = total
    blocks = []
    for q in range(4):
        parts = [sum_ref[pl.ds(c * 4 + q, 32, stride=8), :] for c in range(2)]
        turned = jnp.concatenate(parts, axis=0).T
        own = [turned[i * 16 : (i + 1) * 16, :] for i in range(8)]
        blocks.append(jnp.concatenate(own, axis=1))
    left = jnp.concatenate(split(jnp.concatenate(blocks, axis=0)), axis=0)
    both = dot(left, inv_ref[...])
    result = both[:64] + both[64:]
    for q in range(4):
        out_ref[:, q, :] = result[q * 16 : (q + 1) * 16, :]


VMEM_SPEC = pl.BlockSpec(memory_space=pltpu.VMEM)
SMEM_SPEC = pl.BlockSpec(memory_space=pltpu.SMEM)
HBM_SPEC = pl.BlockSpec(memory_space=pltpu.HBM)


LIMIT = pltpu.CompilerParams(vmem_limit_bytes=24 << 20)


def on_chip(a):
    return pltpu.with_memory_space_constraint(a, pltpu.VMEM)


def off_chip(a):
    return pltpu.with_memory_space_constraint(a, pltpu.HBM)


def local(density, degree_weights, row_orders, target_cycles):
    forward_trig, inverse_trig = trig_tables(256, 512, 256)
    orders_row = row_orders.reshape(1, 256)
    own_orders = lax.dynamic_slice_in_dim(row_orders, lax.axis_index("ord") * 8, 8)
    centers = (jnp.arange(256, dtype=F32) + 0.5) * (math.pi / 256)
    grid = jnp.stack([jnp.cos(centers), jnp.sin(centers), math.pi / 256 * jnp.sin(centers)])

    spectra = pl.pallas_call(
        forward_kernel,
        out_shape=pltpu.HBM((32, 128, 128), BF16),
        in_specs=[HBM_SPEC] * 3,
        out_specs=HBM_SPEC,
        scratch_shapes=[
            pltpu.VMEM((1, 256), jnp.int32),
            pltpu.VMEM((1024, 512), BF16),
            pltpu.VMEM((256, 1024), BF16),
            pltpu.VMEM((8, 128, 512), BF16),
            pltpu.VMEM((32, 128, 128), BF16),
            pltpu.SemaphoreType.DMA((3,)),
            pltpu.SemaphoreType.DMA((2,)),
        ],
        name="forward",
        compiler_params=LIMIT,
    )(off_chip(orders_row), off_chip(density.reshape(1024, 512)), off_chip(jnp.asarray(forward_trig)))
    by_order = lax.all_to_all(spectra, "ord", split_axis=0, concat_axis=0, tiled=True)

    analysis, transfer, inverse_rows = pl.pallas_call(
        table_kernel,
        out_shape=(
            pltpu.HBM((8, 256, 256), BF16),
            pltpu.VMEM((8, 128, 256), BF16),
            pltpu.HBM((512, 512), BF16),
        ),
        in_specs=[SMEM_SPEC] + [VMEM_SPEC] * 5,
        out_specs=(VMEM_SPEC,) * 3,
        scratch_shapes=[pltpu.VMEM((2, 2048, 128), F32), pltpu.VMEM((8, 256, 128), F32)],
        name="tables",
        compiler_params=LIMIT,
    )(own_orders, orders_row, target_cycles.reshape(1, 128), grid, jnp.asarray(inverse_trig),
      degree_weights)

    received = on_chip(by_order.reshape(4096, 128))
    modes = pl.pallas_call(
        mode_kernel,
        out_shape=pltpu.HBM((2048, 128), BF16),
        in_specs=[VMEM_SPEC] * 2,
        out_specs=HBM_SPEC,
        scratch_shapes=[
            pltpu.VMEM((16, 256, 128), BF16),
            pltpu.VMEM((8, 128, 256), BF16),
            pltpu.VMEM((2048, 128), BF16),
            pltpu.SemaphoreType.DMA((2,)),
        ],
        name="modes",
        compiler_params=LIMIT,
    )(received, on_chip(transfer))

    arrived = lax.all_to_all(
        modes.reshape(256, 8, 128), ("band", "ord"), split_axis=0, concat_axis=0, tiled=True
    )
    coeffs = pl.pallas_call(
        coeffs_kernel,
        out_shape=pltpu.VMEM((8, 256, 256), BF16),
        in_specs=[VMEM_SPEC] * 2,
        out_specs=VMEM_SPEC,
        scratch_shapes=[pltpu.VMEM((16, 256, 128), BF16)],
        name="coeffs",
        compiler_params=LIMIT,
    )(received, analysis)
    potential = pl.pallas_call(
        inverse_kernel,
        out_shape=jax.ShapeDtypeStruct((16, 4, 512), F32),
        in_specs=[VMEM_SPEC] * 2,
        out_specs=VMEM_SPEC,
        scratch_shapes=[pltpu.VMEM((256, 128), F32)],
        name="inverse",
        compiler_params=LIMIT,
    )(on_chip(arrived.reshape(2048, 128)), inverse_rows)
    return coeffs.reshape(1, 8, 128, 2, 256), potential


def solution(mesh):
    in_specs = (P("band", None, "ord", None), P("band", None), P(), P())
    out_specs = (P("band", "ord", None, None, None), P("band", "ord", None))
    return jax.shard_map(local, mesh=mesh, in_specs=in_specs, out_specs=out_specs, check_vma=False)
```

```python
import math

import numpy as np
import jax
import jax.numpy as jnp
from jax import lax
from jax.experimental import pallas as pl
from jax.experimental.pallas import tpu as pltpu
from jax.sharding import PartitionSpec as P

F32 = jnp.float32
BF16 = jnp.bfloat16
NN = (((1,), (0,)), ((), ()))
NT = (((1,), (1,)), ((), ()))
TN = (((0,), (0,)), ((), ()))


def dot(a, b, dims=NN):
    return lax.dot_general(a, b, dims, preferred_element_type=F32)


def trig_tables(order_count, lon_count, lat_count):
    turns = np.arange(order_count)[:, None] * np.arange(lon_count)[None, :] % lon_count
    phases = turns * (2.0 * math.pi / lon_count)
    gain = math.sqrt(lat_count * lon_count / (4.0 * math.pi))
    waves = np.concatenate([np.cos(phases), -np.sin(phases)], axis=1)
    forward = waves * (2.0 * math.pi / lon_count * gain)
    twice = np.where(np.arange(order_count) == 0, 1.0, 2.0)[:, None]
    inverse = waves * twice / gain
    kind = jnp.dtype(BF16)
    return forward.astype(np.float32).astype(kind), inverse.astype(np.float32).astype(kind)


def iota(shape, axis):
    return lax.broadcasted_iota(jnp.int32, shape, axis)


def one_hot(hit):
    return jnp.where(hit, 1.0, 0.0).astype(BF16)


def split(a):
    high = a.astype(BF16)
    return high, (a - high.astype(F32)).astype(BF16)


def swap_matrix(outer, inner):
    n = outer * inner
    row, col = iota((n, n), 0), iota((n, n), 1)
    return one_hot(col == (row % inner) * outer + row // inner)


def forward_kernel(orders_hbm, density_hbm, table_hbm, out_hbm,
                   orders_ref, density_ref, table_ref, turned_ref, stack_ref, out_ref,
                   in_sem, out_sem):
    orders_copy = pltpu.make_async_copy(orders_hbm, orders_ref, in_sem.at[0])
    table_copy = pltpu.make_async_copy(table_hbm, table_ref, in_sem.at[1])
    density_copy = pltpu.make_async_copy(density_hbm, density_ref, in_sem.at[2])
    orders_copy.start()
    table_copy.start()
    density_copy.start()
    swap = swap_matrix(8, 32)
    orders_copy.wait()
    hits = jnp.where(iota((256, 256), 0) == orders_ref[...], 1.0, 0.0)
    picks = hits.T.astype(BF16)
    table_copy.wait()
    rows = dot(picks, table_ref[...])
    cos_rows = rows[:, :512].reshape(32, 8, 512)
    sin_rows = rows[:, 512:].reshape(32, 8, 512)
    forward = jnp.stack([cos_rows, sin_rows], axis=1).reshape(512, 512).astype(BF16)
    density_copy.wait()
    for b in range(4):
        part = dot(swap, density_ref[b * 256 : (b + 1) * 256, :]).astype(BF16)
        turned_ref[:, b * 32 : (b + 1) * 32, :] = part.reshape(8, 32, 512)
    sends = []

    def finish(half):
        rows = stack_ref[half * 2048 : (half + 1) * 2048, :].astype(BF16)
        out_ref[half * 16 : (half + 1) * 16] = rows.reshape(16, 128, 128)

    def send(half):
        block = pl.ds(half * 16, 16)
        copy = pltpu.make_async_copy(out_ref.at[block], out_hbm.at[block], out_sem.at[half])
        copy.start()
        sends.append(copy)

    for half in range(2):
        rows = forward[half * 256 : (half + 1) * 256]
        for j in range(0, 8, 2):
            lanes = turned_ref[j : j + 2].reshape(256, 512)
            part = dot(rows, lanes, NT)
            for e in range(2):
                places = pl.ds(half * 2048 + j + e, 256, stride=8)
                stack_ref[places, :] = part[:, e * 128 : (e + 1) * 128]
            if half == 1 and j == 2:
                finish(0)
    send(0)
    finish(1)
    send(1)
    for copy in sends:
        copy.wait()


def table_kernel(own_ref, orders_ref, target_ref, grid_ref, inverse_ref, weights_ref,
                 analysis_ref, transfer_ref, inv_ref, legendre_ref, rows_ref):
    sub = iota((8, 256), 0)
    order = jnp.zeros((8, 256), F32)
    for i in range(8):
        order = jnp.where(sub == i, own_ref[i].astype(F32), order)
    cosines = jnp.broadcast_to(grid_ref[0:1, :], (8, 256))
    log_sines = jnp.log(grid_ref[1:2, :])
    weights = grid_ref[2:3, :]
    steps = iota((8, 256), 1).astype(F32)
    safe = jnp.maximum(steps, 1.0)
    log_terms = jnp.log((2.0 * safe + 1.0) / (2.0 * safe))
    counted = (steps >= 1.0) & (steps <= order)
    gamma = jnp.sum(jnp.where(counted, log_terms, 0.0), axis=1, keepdims=True)
    log_start = 0.5 * (math.log(1.0 / (4.0 * math.pi)) + gamma) + order * log_sines
    shift = jnp.clip(-log_start - 40.0, 0.0, 80.0)
    sectoral = jnp.exp(log_start + shift)
    unshift = jnp.exp(-shift)
    half = order[:, :128]
    half_sq = half * half

    def wide(a):
        return jnp.concatenate([a, a], axis=1)

    def advance(step, carry):
        previous, earlier = carry
        degree = jnp.full((8, 128), step, jnp.int32).astype(F32)
        square = degree * degree
        growth = jnp.sqrt(
            jnp.maximum(4.0 * square - 1.0, 0.0) / jnp.maximum(square - half_sq, 1.0)
        )
        lower = degree - 1.0
        low_sq = lower * lower
        damping = jnp.sqrt(
            jnp.maximum(low_sq - half_sq, 0.0) / jnp.maximum(4.0 * low_sq - 1.0, 1.0)
        )
        grown = wide(growth) * (cosines * previous - wide(damping) * earlier)
        wide_degree = wide(degree)
        current = jnp.where(
            wide_degree < order, 0.0, jnp.where(wide_degree == order, sectoral, grown)
        )
        final = current * unshift
        rows = pl.ds(pl.multiple_of(step * 8, 8), 8)
        legendre_ref[0, rows, :] = final[:, :128]
        legendre_ref[1, rows, :] = final[:, 128:]
        return current, previous

    empty = sectoral * 0.0
    lax.fori_loop(0, 256, advance, (empty, empty), unroll=8)

    hits = jnp.where(iota((256, 128), 0) == target_ref[...], 1.0, 0.0)
    picks = hits.T.astype(BF16)
    for i in range(8):
        halves = [legendre_ref[h, pl.ds(i, 256, stride=8), :] for h in range(2)]
        own = jnp.concatenate(halves, axis=1)
        analysis = (own * weights).astype(BF16)
        synthesis = dot(picks, own.astype(BF16), NT)
        high, low = split(synthesis * weights_ref[...])
        analysis_ref[i] = analysis
        transfer_ref[i] = (dot(high, analysis) + dot(low, analysis)).astype(BF16)

    places = one_hot(iota((256, 256), 0) == orders_ref[...])
    rows = dot(places, inverse_ref[...], TN)
    for c in range(8):
        rows_ref[c] = rows[:, c * 128 : (c + 1) * 128]
    for i in range(8):
        for c in range(8):
            own = rows_ref[c, pl.ds(i, 32, stride=8), :].astype(BF16)
            top = i * 64 + c // 4 * 32
            inv_ref[top : top + 32, c % 4 * 128 : (c % 4 + 1) * 128] = own


def order_spectra(spectra_ref, i):
    parts = []
    for c in range(2):
        top = (c * 8 + i) * 8
        parts.append(spectra_ref[:, top : top + 8, :].reshape(256, 128))
    return jnp.concatenate(parts, axis=1)


def mode_kernel(spectra_ref, transfer_ref, out_hbm, modes_ref, out_ref, out_sem):
    row, col = iota((256, 256), 0), iota((256, 256), 1)
    deal = one_hot(col == (row // 4 % 2) * 128 + row // 8 * 4 + row % 4)
    for i in range(8):
        modes = dot(transfer_ref[i], order_spectra(spectra_ref, i)).astype(BF16)
        modes_ref[:, i * 16 : (i + 1) * 16, :] = modes.reshape(8, 16, 256)
    sends = []
    for b in range(0, 8, 2):
        pair = modes_ref[b : b + 2].reshape(256, 256)
        block = dot(deal, pair, NT).astype(BF16)
        out_ref[b * 256 : (b + 1) * 256, :] = block[:, :128]
        out_ref[(b + 1) * 256 : (b + 2) * 256, :] = block[:, 128:]
        if b in (2, 6):
            half = pl.ds((b - 2) * 256, 1024)
            send = pltpu.make_async_copy(out_ref.at[half], out_hbm.at[half], out_sem.at[b // 4])
            send.start()
            sends.append(send)
    for send in sends:
        send.wait()


def coeffs_kernel(spectra_ref, analysis_ref, out_ref):
    row, col = iota((256, 256), 0), iota((256, 256), 1)
    interleave = one_hot(col == (row % 2) * 128 + row // 2)
    for i in range(8):
        harmonic = dot(analysis_ref[i], order_spectra(spectra_ref, i)).astype(BF16)
        out_ref[i] = dot(interleave, harmonic, NT).astype(BF16)


def inverse_kernel(modes_ref, inv_ref, out_ref, sum_ref):
    total = modes_ref[0:256, :].astype(F32)
    for g in range(1, 8):
        total = total + modes_ref[g * 256 : (g + 1) * 256, :].astype(F32)
    sum_ref[...] = total
    blocks = []
    for q in range(4):
        parts = [sum_ref[pl.ds(c * 4 + q, 32, stride=8), :] for c in range(2)]
        turned = jnp.concatenate(parts, axis=0).T
        own = [turned[i * 16 : (i + 1) * 16, :] for i in range(8)]
        blocks.append(jnp.concatenate(own, axis=1))
    left = jnp.concatenate(split(jnp.concatenate(blocks, axis=0)), axis=0)
    both = dot(left, inv_ref[...])
    result = both[:64] + both[64:]
    for q in range(4):
        out_ref[:, q, :] = result[q * 16 : (q + 1) * 16, :]


VMEM_SPEC = pl.BlockSpec(memory_space=pltpu.VMEM)
SMEM_SPEC = pl.BlockSpec(memory_space=pltpu.SMEM)
HBM_SPEC = pl.BlockSpec(memory_space=pltpu.HBM)


LIMIT = pltpu.CompilerParams(vmem_limit_bytes=24 << 20)


def on_chip(a):
    return pltpu.with_memory_space_constraint(a, pltpu.VMEM)


def off_chip(a):
    return pltpu.with_memory_space_constraint(a, pltpu.HBM)


def local(density, degree_weights, row_orders, target_cycles):
    forward_trig, inverse_trig = trig_tables(256, 512, 256)
    orders_row = row_orders.reshape(1, 256)
    own_orders = lax.dynamic_slice_in_dim(row_orders, lax.axis_index("ord") * 8, 8)
    centers = (jnp.arange(256, dtype=F32) + 0.5) * (math.pi / 256)
    grid = jnp.stack([jnp.cos(centers), jnp.sin(centers), math.pi / 256 * jnp.sin(centers)])

    spectra = pl.pallas_call(
        forward_kernel,
        out_shape=pltpu.HBM((32, 128, 128), BF16),
        in_specs=[HBM_SPEC] * 3,
        out_specs=HBM_SPEC,
        scratch_shapes=[
            pltpu.VMEM((1, 256), jnp.int32),
            pltpu.VMEM((1024, 512), BF16),
            pltpu.VMEM((256, 1024), BF16),
            pltpu.VMEM((8, 128, 512), BF16),
            pltpu.VMEM((4096, 128), F32),
            pltpu.VMEM((32, 128, 128), BF16),
            pltpu.SemaphoreType.DMA((3,)),
            pltpu.SemaphoreType.DMA((2,)),
        ],
        name="forward",
        compiler_params=LIMIT,
    )(off_chip(orders_row), off_chip(density.reshape(1024, 512)), off_chip(jnp.asarray(forward_trig)))
    by_order = lax.all_to_all(spectra, "ord", split_axis=0, concat_axis=0, tiled=True)

    analysis, transfer, inverse_rows = pl.pallas_call(
        table_kernel,
        out_shape=(
            pltpu.HBM((8, 256, 256), BF16),
            pltpu.VMEM((8, 128, 256), BF16),
            pltpu.HBM((512, 512), BF16),
        ),
        in_specs=[SMEM_SPEC] + [VMEM_SPEC] * 5,
        out_specs=(VMEM_SPEC,) * 3,
        scratch_shapes=[pltpu.VMEM((2, 2048, 128), F32), pltpu.VMEM((8, 256, 128), F32)],
        name="tables",
        compiler_params=LIMIT,
    )(own_orders, orders_row, target_cycles.reshape(1, 128), grid, jnp.asarray(inverse_trig),
      degree_weights)

    received = on_chip(by_order)
    modes = pl.pallas_call(
        mode_kernel,
        out_shape=pltpu.HBM((2048, 128), BF16),
        in_specs=[VMEM_SPEC] * 2,
        out_specs=HBM_SPEC,
        scratch_shapes=[
            pltpu.VMEM((8, 128, 256), BF16),
            pltpu.VMEM((2048, 128), BF16),
            pltpu.SemaphoreType.DMA((2,)),
        ],
        name="modes",
        compiler_params=LIMIT,
    )(received, on_chip(transfer))

    arrived = lax.all_to_all(
        modes.reshape(256, 8, 128), ("band", "ord"), split_axis=0, concat_axis=0, tiled=True
    )
    coeffs = pl.pallas_call(
        coeffs_kernel,
        out_shape=pltpu.VMEM((8, 256, 256), BF16),
        in_specs=[VMEM_SPEC] * 2,
        out_specs=VMEM_SPEC,
        name="coeffs",
        compiler_params=LIMIT,
    )(received, analysis)
    potential = pl.pallas_call(
        inverse_kernel,
        out_shape=jax.ShapeDtypeStruct((16, 4, 512), F32),
        in_specs=[VMEM_SPEC] * 2,
        out_specs=VMEM_SPEC,
        scratch_shapes=[pltpu.VMEM((256, 128), F32)],
        name="inverse",
        compiler_params=LIMIT,
    )(on_chip(arrived.reshape(2048, 128)), inverse_rows)
    return coeffs.reshape(1, 8, 128, 2, 256), potential


def solution(mesh):
    in_specs = (P("band", None, "ord", None), P("band", None), P(), P())
    out_specs = (P("band", "ord", None, None, None), P("band", "ord", None))
    return jax.shard_map(local, mesh=mesh, in_specs=in_specs, out_specs=out_specs, check_vma=False)
```

```python
import math

import numpy as np
import jax
import jax.numpy as jnp
from jax import lax
from jax.experimental import pallas as pl
from jax.experimental.pallas import tpu as pltpu
from jax.sharding import PartitionSpec as P

F32 = jnp.float32
BF16 = jnp.bfloat16
NN = (((1,), (0,)), ((), ()))
NT = (((1,), (1,)), ((), ()))
TN = (((0,), (0,)), ((), ()))


def dot(a, b, dims=NN):
    return lax.dot_general(a, b, dims, preferred_element_type=F32)


def trig_tables(order_count, lon_count, lat_count):
    turns = np.arange(order_count)[:, None] * np.arange(lon_count)[None, :] % lon_count
    phases = turns * (2.0 * math.pi / lon_count)
    gain = math.sqrt(lat_count * lon_count / (4.0 * math.pi))
    waves = np.concatenate([np.cos(phases), -np.sin(phases)], axis=1)
    forward = waves * (2.0 * math.pi / lon_count * gain)
    twice = np.where(np.arange(order_count) == 0, 1.0, 2.0)[:, None]
    inverse = waves * twice / gain
    kind = jnp.dtype(BF16)
    return forward.astype(np.float32).astype(kind), inverse.astype(np.float32).astype(kind)


def iota(shape, axis):
    return lax.broadcasted_iota(jnp.int32, shape, axis)


def one_hot(hit):
    return jnp.where(hit, 1.0, 0.0).astype(BF16)


def split(a):
    high = a.astype(BF16)
    return high, (a - high.astype(F32)).astype(BF16)


def swap_matrix(outer, inner):
    n = outer * inner
    row, col = iota((n, n), 0), iota((n, n), 1)
    return one_hot(col == (row % inner) * outer + row // inner)


def forward_kernel(orders_hbm, density_hbm, table_hbm, out_hbm,
                   orders_ref, density_ref, table_ref, turned_ref, stack_ref, out_ref,
                   in_sem, out_sem):
    orders_copy = pltpu.make_async_copy(orders_hbm, orders_ref, in_sem.at[0])
    table_copy = pltpu.make_async_copy(table_hbm, table_ref, in_sem.at[1])
    density_copy = pltpu.make_async_copy(density_hbm, density_ref, in_sem.at[2])
    orders_copy.start()
    table_copy.start()
    density_copy.start()
    swap = swap_matrix(8, 32)
    orders_copy.wait()
    hits = jnp.where(iota((256, 256), 0) == orders_ref[...], 1.0, 0.0)
    picks = hits.T.astype(BF16)
    table_copy.wait()
    rows = dot(picks, table_ref[...])
    cos_rows = rows[:, :512].reshape(32, 8, 512)
    sin_rows = rows[:, 512:].reshape(32, 8, 512)
    forward = jnp.stack([cos_rows, sin_rows], axis=1).reshape(512, 512).astype(BF16)
    density_copy.wait()
    for b in range(4):
        part = dot(swap, density_ref[b * 256 : (b + 1) * 256, :]).astype(BF16)
        turned_ref[:, b * 32 : (b + 1) * 32, :] = part.reshape(8, 32, 512)
    sends = []

    def finish(half):
        rows = stack_ref[half * 2048 : (half + 1) * 2048, :].astype(BF16)
        out_ref[half * 16 : (half + 1) * 16] = rows.reshape(16, 128, 128)

    def send(half):
        block = pl.ds(half * 16, 16)
        copy = pltpu.make_async_copy(out_ref.at[block], out_hbm.at[block], out_sem.at[half])
        copy.start()
        sends.append(copy)

    for half in range(2):
        rows = forward[half * 256 : (half + 1) * 256]
        for j in range(0, 8, 2):
            lanes = turned_ref[j : j + 2].reshape(256, 512)
            part = dot(rows, lanes, NT)
            for e in range(2):
                places = pl.ds(half * 2048 + j + e, 256, stride=8)
                stack_ref[places, :] = part[:, e * 128 : (e + 1) * 128]
            if half == 1 and j == 2:
                finish(0)
    send(0)
    finish(1)
    send(1)
    for copy in sends:
        copy.wait()


def table_kernel(own_ref, orders_ref, target_ref, grid_ref, inverse_ref, weights_ref,
                 analysis_ref, transfer_ref, inv_ref, legendre_ref, rows_ref):
    sub = iota((8, 256), 0)
    order = jnp.zeros((8, 256), F32)
    for i in range(8):
        order = jnp.where(sub == i, own_ref[i].astype(F32), order)
    cosines = jnp.broadcast_to(grid_ref[0:1, :], (8, 256))
    log_sines = jnp.log(grid_ref[1:2, :])
    weights = grid_ref[2:3, :]
    steps = iota((8, 256), 1).astype(F32)
    safe = jnp.maximum(steps, 1.0)
    log_terms = jnp.log((2.0 * safe + 1.0) / (2.0 * safe))
    counted = (steps >= 1.0) & (steps <= order)
    gamma = jnp.sum(jnp.where(counted, log_terms, 0.0), axis=1, keepdims=True)
    log_start = 0.5 * (math.log(1.0 / (4.0 * math.pi)) + gamma) + order * log_sines
    shift = jnp.clip(-log_start - 40.0, 0.0, 80.0)
    sectoral = jnp.exp(log_start + shift)
    unshift = jnp.exp(-shift)
    half = order[:, :128]
    half_sq = half * half

    def wide(a):
        return jnp.concatenate([a, a], axis=1)

    def advance(step, carry):
        previous, earlier = carry
        degree = jnp.full((8, 128), step, jnp.int32).astype(F32)
        square = degree * degree
        growth = jnp.sqrt(
            jnp.maximum(4.0 * square - 1.0, 0.0) / jnp.maximum(square - half_sq, 1.0)
        )
        lower = degree - 1.0
        low_sq = lower * lower
        damping = jnp.sqrt(
            jnp.maximum(low_sq - half_sq, 0.0) / jnp.maximum(4.0 * low_sq - 1.0, 1.0)
        )
        grown = wide(growth) * (cosines * previous - wide(damping) * earlier)
        wide_degree = wide(degree)
        current = jnp.where(
            wide_degree < order, 0.0, jnp.where(wide_degree == order, sectoral, grown)
        )
        final = current * unshift
        rows = pl.ds(pl.multiple_of(step * 8, 8), 8)
        legendre_ref[0, rows, :] = final[:, :128]
        legendre_ref[1, rows, :] = final[:, 128:]
        return current, previous

    empty = sectoral * 0.0
    lax.fori_loop(0, 256, advance, (empty, empty), unroll=8)

    hits = jnp.where(iota((256, 128), 0) == target_ref[...], 1.0, 0.0)
    picks = hits.T.astype(BF16)
    for i in range(8):
        halves = [legendre_ref[h, pl.ds(i, 256, stride=8), :] for h in range(2)]
        own = jnp.concatenate(halves, axis=1)
        analysis = (own * weights).astype(BF16)
        synthesis = dot(picks, own.astype(BF16), NT)
        high, low = split(synthesis * weights_ref[...])
        analysis_ref[i] = analysis
        transfer_ref[i] = (dot(high, analysis) + dot(low, analysis)).astype(BF16)

    places = one_hot(iota((256, 256), 0) == orders_ref[...])
    rows = dot(places, inverse_ref[...], TN)
    for c in range(8):
        rows_ref[c] = rows[:, c * 128 : (c + 1) * 128]
    for i in range(8):
        for c in range(8):
            own = rows_ref[c, pl.ds(i, 32, stride=8), :].astype(BF16)
            top = i * 64 + c // 4 * 32
            inv_ref[top : top + 32, c % 4 * 128 : (c % 4 + 1) * 128] = own


def order_spectra(spectra_ref, i):
    parts = []
    for c in range(2):
        top = (c * 8 + i) * 8
        parts.append(spectra_ref[:, top : top + 8, :].reshape(256, 128))
    return jnp.concatenate(parts, axis=1)


def mode_kernel(spectra_ref, transfer_ref, out_hbm, modes_ref, out_ref, out_sem):
    row, col = iota((256, 256), 0), iota((256, 256), 1)
    deal = one_hot(col == (row // 4 % 2) * 128 + row // 8 * 4 + row % 4)
    for i in range(8):
        modes = dot(transfer_ref[i], order_spectra(spectra_ref, i)).astype(BF16)
        modes_ref[:, i * 16 : (i + 1) * 16, :] = modes.reshape(8, 16, 256)
    sends = []
    for b in range(0, 8, 2):
        pair = modes_ref[b : b + 2].reshape(256, 256)
        block = dot(deal, pair, NT).astype(BF16)
        out_ref[b * 256 : (b + 1) * 256, :] = block[:, :128]
        out_ref[(b + 1) * 256 : (b + 2) * 256, :] = block[:, 128:]
        if b in (2, 6):
            half = pl.ds((b - 2) * 256, 1024)
            send = pltpu.make_async_copy(out_ref.at[half], out_hbm.at[half], out_sem.at[b // 4])
            send.start()
            sends.append(send)
    for send in sends:
        send.wait()


def coeffs_kernel(spectra_ref, analysis_ref, out_ref):
    row, col = iota((256, 256), 0), iota((256, 256), 1)
    interleave = one_hot(col == (row % 2) * 128 + row // 2)
    for i in range(8):
        harmonic = dot(analysis_ref[i], order_spectra(spectra_ref, i)).astype(BF16)
        out_ref[i] = dot(interleave, harmonic, NT).astype(BF16)


def inverse_kernel(modes_ref, inv_ref, out_ref, sum_ref):
    total = modes_ref[0:256, :].astype(F32)
    for g in range(1, 8):
        total = total + modes_ref[g * 256 : (g + 1) * 256, :].astype(F32)
    sum_ref[...] = total
    blocks = []
    for q in range(4):
        parts = [sum_ref[pl.ds(c * 4 + q, 32, stride=8), :] for c in range(2)]
        turned = jnp.concatenate(parts, axis=0).T
        own = [turned[i * 16 : (i + 1) * 16, :] for i in range(8)]
        blocks.append(jnp.concatenate(own, axis=1))
    left = jnp.concatenate(split(jnp.concatenate(blocks, axis=0)), axis=0)
    both = dot(left, inv_ref[...])
    result = both[:64] + both[64:]
    for q in range(4):
        out_ref[:, q, :] = result[q * 16 : (q + 1) * 16, :]


VMEM_SPEC = pl.BlockSpec(memory_space=pltpu.VMEM)
SMEM_SPEC = pl.BlockSpec(memory_space=pltpu.SMEM)
HBM_SPEC = pl.BlockSpec(memory_space=pltpu.HBM)


LIMIT = pltpu.CompilerParams(vmem_limit_bytes=24 << 20)
SPREAD = pltpu.CompilerParams(
    vmem_limit_bytes=24 << 20
)


def on_chip(a):
    return pltpu.with_memory_space_constraint(a, pltpu.VMEM)


def off_chip(a):
    return pltpu.with_memory_space_constraint(a, pltpu.HBM)


def local(density, degree_weights, row_orders, target_cycles):
    forward_trig, inverse_trig = trig_tables(256, 512, 256)
    orders_row = row_orders.reshape(1, 256)
    own_orders = lax.dynamic_slice_in_dim(row_orders, lax.axis_index("ord") * 8, 8)
    centers = (jnp.arange(256, dtype=F32) + 0.5) * (math.pi / 256)
    grid = jnp.stack([jnp.cos(centers), jnp.sin(centers), math.pi / 256 * jnp.sin(centers)])

    spectra = pl.pallas_call(
        forward_kernel,
        out_shape=pltpu.HBM((32, 128, 128), BF16),
        in_specs=[HBM_SPEC] * 3,
        out_specs=HBM_SPEC,
        scratch_shapes=[
            pltpu.VMEM((1, 256), jnp.int32),
            pltpu.VMEM((1024, 512), BF16),
            pltpu.VMEM((256, 1024), BF16),
            pltpu.VMEM((8, 128, 512), BF16),
            pltpu.VMEM((4096, 128), F32),
            pltpu.VMEM((32, 128, 128), BF16),
            pltpu.SemaphoreType.DMA((3,)),
            pltpu.SemaphoreType.DMA((2,)),
        ],
        name="forward",
        compiler_params=SPREAD,
    )(off_chip(orders_row), off_chip(density.reshape(1024, 512)), off_chip(jnp.asarray(forward_trig)))
    by_order = lax.all_to_all(spectra, "ord", split_axis=0, concat_axis=0, tiled=True)

    analysis, transfer, inverse_rows = pl.pallas_call(
        table_kernel,
        out_shape=(
            pltpu.HBM((8, 256, 256), BF16),
            pltpu.VMEM((8, 128, 256), BF16),
            pltpu.HBM((512, 512), BF16),
        ),
        in_specs=[SMEM_SPEC] + [VMEM_SPEC] * 5,
        out_specs=(VMEM_SPEC,) * 3,
        scratch_shapes=[pltpu.VMEM((2, 2048, 128), F32), pltpu.VMEM((8, 256, 128), F32)],
        name="tables",
        compiler_params=LIMIT,
    )(own_orders, orders_row, target_cycles.reshape(1, 128), grid, jnp.asarray(inverse_trig),
      degree_weights)

    received = on_chip(by_order)
    modes = pl.pallas_call(
        mode_kernel,
        out_shape=pltpu.HBM((2048, 128), BF16),
        in_specs=[VMEM_SPEC] * 2,
        out_specs=HBM_SPEC,
        scratch_shapes=[
            pltpu.VMEM((8, 128, 256), BF16),
            pltpu.VMEM((2048, 128), BF16),
            pltpu.SemaphoreType.DMA((2,)),
        ],
        name="modes",
        compiler_params=LIMIT,
    )(received, on_chip(transfer))

    arrived = lax.all_to_all(
        modes.reshape(256, 8, 128), ("band", "ord"), split_axis=0, concat_axis=0, tiled=True
    )
    coeffs = pl.pallas_call(
        coeffs_kernel,
        out_shape=pltpu.VMEM((8, 256, 256), BF16),
        in_specs=[VMEM_SPEC] * 2,
        out_specs=VMEM_SPEC,
        name="coeffs",
        compiler_params=LIMIT,
    )(received, analysis)
    potential = pl.pallas_call(
        inverse_kernel,
        out_shape=jax.ShapeDtypeStruct((16, 4, 512), F32),
        in_specs=[VMEM_SPEC] * 2,
        out_specs=VMEM_SPEC,
        scratch_shapes=[pltpu.VMEM((256, 128), F32)],
        name="inverse",
        compiler_params=LIMIT,
    )(on_chip(arrived.reshape(2048, 128)), inverse_rows)
    return coeffs.reshape(1, 8, 128, 2, 256), potential


def solution(mesh):
    in_specs = (P("band", None, "ord", None), P("band", None), P(), P())
    out_specs = (P("band", "ord", None, None, None), P("band", "ord", None))
    return jax.shard_map(local, mesh=mesh, in_specs=in_specs, out_specs=out_specs, check_vma=False)
```
